32 devices in a mesh: rep: 8 (over y, x, core), cp: 4 (over z).
Axes of the slice: x: 2, y: 2, z: 4, core: 2. Of those that a mesh axis runs over, the one named last changes fastest.
Arguments:
- block_input: bfloat16 [4096, 768], P(('rep', 'cp')), may hold values from -6 to 6
- qkv_weight: bfloat16 [768, 2304], P('cp'), may hold values from -4 to 4
- qkv_bias: bfloat16 [2304], P('cp'), may hold values from -3 to 3
- proj_weight: bfloat16 [768, 768], P('cp'), may hold values from -2.5 to 2.5
- proj_bias: bfloat16 [768], P('cp'), may hold values from -3 to 3
- up_weight: bfloat16 [768, 3072], P('cp'), may hold values from -0.21875 to 0.21875
- up_bias: bfloat16 [3072], P('cp'), may hold values from -3 to 3
- down_weight: bfloat16 [3072, 768], P('cp'), may hold values from -0.109375 to 0.109375
- down_bias: bfloat16 [768], P('cp'), may hold values from -3 to 3
- attention_gain: bfloat16 [768], P('cp'), may hold values from 0.099609375 to 1.8984375
- attention_shift: bfloat16 [768], P('cp'), may hold values from -3 to 3
- feed_gain: bfloat16 [768], P('cp'), may hold values from 0.099609375 to 1.8984375
- feed_shift: bfloat16 [768], P('cp'), may hold values from -3 to 3
- out_cotangent: bfloat16 [4096, 768], P(('rep', 'cp')), may hold values from -6 to 6
Outputs:
- block_output: bfloat16 [4096, 768], P(('rep', 'cp'))
- input_grad: float32 [4096, 768], P(('rep', 'cp'))
- qkv_weight_grad: float32 [768, 2304], P('cp')
- qkv_bias_grad: float32 [2304], P('cp')
- proj_weight_grad: float32 [768, 768], P('cp')
- proj_bias_grad: float32 [768], P('cp')
- up_weight_grad: float32 [768, 3072], P('cp')
- up_bias_grad: float32 [3072], P('cp')
- down_weight_grad: float32 [3072, 768], P('cp')
- down_bias_grad: float32 [768], P('cp')
- attention_gain_grad: float32 [768], P('cp')
- attention_shift_grad: float32 [768], P('cp')
- feed_gain_grad: float32 [768], P('cp')
- feed_shift_grad: float32 [768], P('cp')
The draws below stay inside these ranges and needn't reach their ends.
All inputs are finite; a program needn't handle non-finite values.
Results may differ from the reference program's by a relative error of at most 0.013.
Values may be sent and summed in bfloat16 or wider, within the bound.
A program may use at most 128 MiB of HBM per device.

```python
import jax
import jax.numpy as jnp
from jax import lax

D = 768
HEADS = 12
HEAD = 64
ROT = 16
FF = 3072
SEQ = 512
TOKENS = 4096


def draw_qkv_weight(key, part):
    base = jnp.clip(jax.random.normal(key, (D, 3 * D), jnp.float32), -6.0, 6.0) * D ** (-0.5)
    return base.astype(jnp.bfloat16)


def levels(own_key, shape, split, low, top_value):
    def one(position, blocks):
        heights = jax.random.uniform(jax.random.fold_in(jax.random.fold_in(own_key, 6), position), (blocks,), jnp.float32, low / len(split), top_value / len(split))
        return jnp.repeat(jnp.exp(heights), shape[position] // blocks).reshape((-1,) + (1,) * (len(shape) - position - 1))

    gain = one(*split[0])
    for cut in split[1:]:
        gain = gain * one(*cut)
    return gain


def normal_values(own_key, extent, spread, reach, split=(), kind=jnp.bfloat16):
    values = jax.random.normal(own_key, extent, jnp.float32) * spread
    if len(split) > 0:
        values = levels(own_key, extent, split, -0.22, 0.18) * values
    return jnp.clip(values, min=-reach, max=reach).astype(kind)


def setup_inputs(seed: int = 0) -> dict:
    splits = jax.random.split(jax.random.key(seed), 15)
    block_input = normal_values(splits[0], (TOKENS, D), 1.0, 6.0, ((0, 32),))
    qkv_weight = draw_qkv_weight(jax.random.fold_in(splits[14], 71), 0)
    qkv_bias = normal_values(splits[2], (3 * D,), 0.5, 3.0, ((0, 4),))
    proj_weight = normal_values(splits[3], (D, D), (max(1, 4 * D // SEQ)) ** -0.5, 2.5, ((0, 4),))
    proj_bias = normal_values(splits[4], (D,), 0.5, 3.0, ((0, 4),))
    up_weight = normal_values(splits[5], (D, FF), D ** -0.5, 0.21875, ((0, 4),))
    up_bias = normal_values(splits[6], (FF,), 0.5, 3.0, ((0, 4),))
    down_weight = normal_values(splits[7], (FF, D), FF ** -0.5, 0.109375, ((0, 4),))
    down_bias = normal_values(splits[8], (D,), 0.5, 3.0, ((0, 4),))
    attention_gain = jnp.clip(1.0 + 0.18 * jax.random.normal(splits[9], (D,), jnp.float32), 0.099609375, 1.8984375).astype(jnp.bfloat16)
    attention_shift = normal_values(splits[10], (D,), 0.5, 3.0, ((0, 4),))
    feed_gain = jnp.clip(1.0 + 0.18 * jax.random.normal(splits[11], (D,), jnp.float32), 0.099609375, 1.8984375).astype(jnp.bfloat16)
    feed_shift = normal_values(splits[12], (D,), 0.5, 3.0, ((0, 4),))
    out_cotangent = normal_values(splits[13], (TOKENS, D), 1.0, 6.0, ((0, 32),))
    return {"block_input": block_input, "qkv_weight": qkv_weight, "qkv_bias": qkv_bias, "proj_weight": proj_weight, "proj_bias": proj_bias, "up_weight": up_weight, "up_bias": up_bias, "down_weight": down_weight, "down_bias": down_bias, "attention_gain": attention_gain, "attention_shift": attention_shift, "feed_gain": feed_gain, "feed_shift": feed_shift, "out_cotangent": out_cotangent}


EPSILON = 1e-05
ROOT_HALF = 0.7071067811865476
INV_ROOT_TWO_PI = 0.3989422804014327

def layer_norm(inputs, norm_gain, norm_shift):
    center = inputs - lax.optimization_barrier(jnp.mean(inputs, axis=-1, keepdims=True))
    inverse = lax.rsqrt(lax.optimization_barrier(jnp.mean(center * center, axis=-1, keepdims=True)) + EPSILON)
    normed = center * inverse
    return (normed * norm_gain.astype(jnp.float32) + norm_shift.astype(jnp.float32), normed, inverse)

def norm_back(upstream, normed, inverse, norm_gain):
    scaled = upstream * norm_gain.astype(jnp.float32)
    return inverse * (scaled - lax.optimization_barrier(jnp.mean(scaled, axis=-1, keepdims=True)) - normed * lax.optimization_barrier(jnp.mean(scaled * normed, axis=-1, keepdims=True)))

def rotary_tables(positions):
    half_rot = ROT // 2
    inverse_freq = 1.0 / 10000.0 ** (jnp.arange(half_rot, dtype=jnp.float32) * (2.0 / ROT))
    angles = positions.astype(jnp.float32)[:, None] * inverse_freq[None, :]
    cos_table = jnp.concatenate([jnp.cos(angles), jnp.cos(angles)], axis=-1)
    sin_table = jnp.concatenate([jnp.sin(angles), jnp.sin(angles)], axis=-1)
    return (cos_table, sin_table)

def rotate(heads_in, cos_table, sin_table):
    half_rot = ROT // 2
    rotary_part = heads_in[..., :ROT]
    turned = jnp.concatenate([-rotary_part[..., half_rot:], rotary_part[..., :half_rot]], axis=-1)
    rotated = rotary_part * cos_table[:, None, :] + turned * sin_table[:, None, :]
    return jnp.concatenate([rotated, heads_in[..., ROT:]], axis=-1)

def rotate_back(heads_grad, cos_table, sin_table):
    half_rot = ROT // 2
    sined = heads_grad[..., :ROT] * sin_table[:, None, :]
    swapped = jnp.concatenate([sined[..., half_rot:], -sined[..., :half_rot]], axis=-1)
    rotated = heads_grad[..., :ROT] * cos_table[:, None, :] + swapped
    return jnp.concatenate([rotated, heads_grad[..., ROT:]], axis=-1)

def gelu_slope(preact):
    return 0.5 * (1.0 + lax.erf(preact * ROOT_HALF)) + preact * jnp.exp(-0.5 * preact * preact) * INV_ROOT_TWO_PI

def reference(block_input, qkv_weight, qkv_bias, proj_weight, proj_bias, up_weight, up_bias, down_weight, down_bias, attention_gain, attention_shift, feed_gain, feed_shift, out_cotangent):
    score_scale = HEAD ** (-0.5)
    positions = jnp.arange(SEQ, dtype=jnp.int32)
    cos_table, sin_table = rotary_tables(positions)
    causal = positions[:, None] >= positions[None, :]
    widths = jnp.float32

    def one_sequence(totals, inputs):
        seq_input, seq_cot = inputs
        widened = seq_input.astype(jnp.float32)
        norm_one, normed_one, inverse_one = layer_norm(widened, attention_gain, attention_shift)
        norm_two, normed_two, inverse_two = layer_norm(widened, feed_gain, feed_shift)
        attn_in = norm_one.astype(jnp.bfloat16)
        feed_in = norm_two.astype(jnp.bfloat16)
        joined_out = jnp.dot(attn_in, qkv_weight, preferred_element_type=jnp.float32) + qkv_bias.astype(jnp.float32)
        queries = rotate(joined_out[:, :D].reshape(SEQ, HEADS, HEAD), cos_table, sin_table).astype(jnp.bfloat16)
        keys_all = rotate(joined_out[:, D:2 * D].reshape(SEQ, HEADS, HEAD), cos_table, sin_table).astype(jnp.bfloat16)
        values_all = joined_out[:, 2 * D:].reshape(SEQ, HEADS, HEAD).astype(jnp.bfloat16)
        scores = jnp.einsum('thd,shd->hts', queries.astype(widths), keys_all.astype(widths)) * score_scale
        scores = jnp.where(causal[None], scores, -jnp.inf)
        top_score = lax.optimization_barrier(jnp.max(scores, axis=-1, keepdims=True))
        log_total = top_score + jnp.log(lax.optimization_barrier(jnp.sum(jnp.exp(scores - top_score), axis=-1, keepdims=True)))
        exact_probs = jnp.exp(scores - log_total)
        probs_low = exact_probs.astype(jnp.bfloat16)
        context = jnp.einsum('hts,shd->thd', probs_low.astype(widths), values_all.astype(widths)).reshape(SEQ, D).astype(jnp.bfloat16)
        attention_out = jnp.dot(context, proj_weight, preferred_element_type=jnp.float32) + proj_bias.astype(jnp.float32)
        pre_act = jnp.dot(feed_in, up_weight, preferred_element_type=jnp.float32) + up_bias.astype(jnp.float32)
        activated = (0.5 * pre_act * (1.0 + lax.erf(pre_act * ROOT_HALF))).astype(jnp.bfloat16)
        feed_out = jnp.dot(activated, down_weight, preferred_element_type=jnp.float32) + down_bias.astype(jnp.float32)
        result = (widened + attention_out + feed_out).astype(jnp.bfloat16)
        upstream = seq_cot.astype(jnp.float32)
        bias_sum = lax.optimization_barrier(jnp.sum(upstream, axis=0))
        down_grad = jnp.dot(activated.T, seq_cot, preferred_element_type=jnp.float32)
        pre_grad = jnp.dot(seq_cot, down_weight.T, preferred_element_type=jnp.float32) * gelu_slope(pre_act)
        pre_low = pre_grad.astype(jnp.bfloat16)
        up_grad = jnp.dot(feed_in.T, pre_low, preferred_element_type=jnp.float32)
        up_bgrad = lax.optimization_barrier(jnp.sum(pre_grad, axis=0))
        feed_in_grad = jnp.dot(pre_low, up_weight.T, preferred_element_type=jnp.float32)
        proj_grad = jnp.dot(context.T, seq_cot, preferred_element_type=jnp.float32)
        context_grad = jnp.dot(seq_cot, proj_weight.T, preferred_element_type=jnp.float32).astype(jnp.bfloat16).reshape(SEQ, HEADS, HEAD)
        row_dots = lax.optimization_barrier(jnp.sum(context_grad.astype(widths) * context.reshape(SEQ, HEADS, HEAD).astype(widths), axis=-1)).T
        probs_grad = jnp.einsum('thd,shd->hts', context_grad.astype(widths), values_all.astype(widths))
        score_grad = (exact_probs * (probs_grad - row_dots[:, :, None]) * score_scale).astype(jnp.bfloat16)
        query_grad = jnp.einsum('hts,shd->thd', score_grad.astype(widths), keys_all.astype(widths))
        key_grad = jnp.einsum('hts,thd->shd', score_grad.astype(widths), queries.astype(widths))
        value_grad = jnp.einsum('hts,thd->shd', probs_low.astype(widths), context_grad.astype(widths))
        joined_grad = jnp.concatenate([rotate_back(query_grad, cos_table, sin_table).reshape(SEQ, D), rotate_back(key_grad, cos_table, sin_table).reshape(SEQ, D), value_grad.reshape(SEQ, D)], axis=1)
        joined_low = joined_grad.astype(jnp.bfloat16)
        qkv_grad = jnp.dot(attn_in.T, joined_low, preferred_element_type=jnp.float32)
        qkv_bgrad = lax.optimization_barrier(jnp.sum(joined_grad, axis=0))
        attn_in_grad = jnp.dot(joined_low, qkv_weight.T, preferred_element_type=jnp.float32)
        input_grad = upstream + norm_back(attn_in_grad, normed_one, inverse_one, attention_gain) + norm_back(feed_in_grad, normed_two, inverse_two, feed_gain)
        terms = (qkv_grad, qkv_bgrad, proj_grad, bias_sum, up_grad, up_bgrad, down_grad, bias_sum, lax.optimization_barrier(jnp.sum(attn_in_grad * normed_one, axis=0)), lax.optimization_barrier(jnp.sum(attn_in_grad, axis=0)), lax.optimization_barrier(jnp.sum(feed_in_grad * normed_two, axis=0)), lax.optimization_barrier(jnp.sum(feed_in_grad, axis=0)))
        totals = jax.tree.map(jnp.add, totals, terms)
        return (totals, (result, input_grad))
    params = (qkv_weight, qkv_bias, proj_weight, proj_bias, up_weight, up_bias, down_weight, down_bias, attention_gain, attention_shift, feed_gain, feed_shift)
    starting = tuple((jnp.zeros(member.shape, jnp.float32) for member in params))
    seq_count = TOKENS // SEQ
    totals, (outputs, grads) = lax.scan(one_sequence, starting, (block_input.reshape(seq_count, SEQ, D), out_cotangent.reshape(seq_count, SEQ, D)))
    return (outputs.reshape(TOKENS, D), grads.reshape(TOKENS, D), totals[0], totals[1], totals[2], totals[3], totals[4], totals[5], totals[6], totals[7], totals[8], totals[9], totals[10], totals[11])
```

```python
import jax
import jax.numpy as jnp
from jax import lax
from jax.sharding import PartitionSpec as P

HEAD = 64
ROT = 16


EPSILON = 1e-05
ROOT_HALF = 0.7071067811865476
INV_ROOT_TWO_PI = 0.3989422804014327


def layer_norm(inputs, norm_gain, norm_shift):
    center = inputs - jnp.mean(inputs, axis=-1, keepdims=True)
    inverse = lax.rsqrt(jnp.mean(center * center, axis=-1, keepdims=True) + EPSILON)
    normed = center * inverse
    return (
        normed * norm_gain.astype(jnp.float32) + norm_shift.astype(jnp.float32),
        normed,
        inverse,
    )


def norm_back(upstream, normed, inverse, norm_gain):
    scaled = upstream * norm_gain.astype(jnp.float32)
    return inverse * (
        scaled
        - jnp.mean(scaled, axis=-1, keepdims=True)
        - normed * jnp.mean(scaled * normed, axis=-1, keepdims=True)
    )


def rotary_tables(positions):
    half_rot = ROT // 2
    inverse_freq = 1.0 / 10000.0 ** (jnp.arange(half_rot, dtype=jnp.float32) * (2.0 / ROT))
    angles = positions.astype(jnp.float32)[:, None] * inverse_freq[None, :]
    cos_table = jnp.concatenate([jnp.cos(angles), jnp.cos(angles)], axis=-1)
    sin_table = jnp.concatenate([jnp.sin(angles), jnp.sin(angles)], axis=-1)
    return (cos_table, sin_table)


def rotate(heads_in, cos_table, sin_table):
    half_rot = ROT // 2
    rotary_part = heads_in[..., :ROT]
    turned = jnp.concatenate([-rotary_part[..., half_rot:], rotary_part[..., :half_rot]], axis=-1)
    rotated = rotary_part * cos_table[:, None, :] + turned * sin_table[:, None, :]
    return jnp.concatenate([rotated, heads_in[..., ROT:]], axis=-1)


def rotate_back(heads_grad, cos_table, sin_table):
    half_rot = ROT // 2
    sined = heads_grad[..., :ROT] * sin_table[:, None, :]
    swapped = jnp.concatenate([sined[..., half_rot:], -sined[..., :half_rot]], axis=-1)
    rotated = heads_grad[..., :ROT] * cos_table[:, None, :] + swapped
    return jnp.concatenate([rotated, heads_grad[..., ROT:]], axis=-1)


def gelu_slope(preact):
    return (
        0.5 * (1.0 + lax.erf(preact * ROOT_HALF))
        + preact * jnp.exp(-0.5 * preact * preact) * INV_ROOT_TWO_PI
    )


def body(
    block_input,
    qkv_weight,
    qkv_bias,
    proj_weight,
    proj_bias,
    up_weight,
    up_bias,
    down_weight,
    down_bias,
    attention_gain,
    attention_shift,
    feed_gain,
    feed_shift,
    out_cotangent,
):
    f32, bf16 = jnp.float32, jnp.bfloat16
    group = lax.axis_size("cp")
    reps = lax.axis_size("rep")
    rank = lax.axis_index("cp")
    rows, width = block_input.shape
    own = width // group
    heads = own // HEAD
    total_rows = rows * group
    hidden = up_weight.shape[1] // group
    qkv_cols = 3 * own
    part_cols = qkv_cols + hidden
    score_scale = HEAD ** (-0.5)

    small = jnp.concatenate(
        [qkv_bias, proj_bias, down_bias, attention_gain, attention_shift, feed_gain, feed_shift]
    )
    small_rows = -(-small.shape[0] // width)
    small_block = jnp.pad(small, (0, small_rows * width - small.shape[0])).reshape(
        small_rows, width
    )
    packed = lax.all_gather(
        jnp.concatenate([block_input, out_cotangent, small_block], axis=0), "cp", axis=0
    )
    tokens = packed[:, :rows].reshape(total_rows, width)
    cotangent = packed[:, rows : 2 * rows].reshape(total_rows, width)
    small_all = packed[:, 2 * rows :].reshape(group, small_rows * width)
    joined_offset_all = small_all[:, :qkv_cols].reshape(group * qkv_cols)
    joined_offset = lax.dynamic_slice_in_dim(
        joined_offset_all.reshape(3, group, own), rank, 1, axis=1
    ).reshape(qkv_cols)
    proj_offset, down_offset, gain_one, shift_one, gain_two, shift_two = (
        small_all[:, qkv_cols + i * own : qkv_cols + (i + 1) * own].reshape(width)
        for i in range(6)
    )

    stripes = jnp.concatenate(
        [
            qkv_weight.reshape(own, 3, group, own).transpose(0, 2, 1, 3).reshape(own, group, -1),
            up_weight.reshape(own, group, hidden),
        ],
        axis=2,
    ).reshape(reps, own // reps, group, part_cols)
    mine = lax.dynamic_index_in_dim(stripes, lax.axis_index("rep"), 0, keepdims=False)
    mine = lax.all_to_all(mine.transpose(1, 0, 2), "cp", 0, 0)
    weights = lax.all_gather(mine, "rep", axis=0)
    weights = weights.transpose(1, 0, 2, 3).reshape(width, part_cols)
    joined_matrix = weights[:, :qkv_cols]
    up_matrix = weights[:, qkv_cols:]

    positions = jnp.arange(total_rows, dtype=jnp.int32)
    cos_table, sin_table = rotary_tables(positions)
    widened = tokens.astype(f32)
    center = widened - jnp.mean(widened, axis=-1, keepdims=True)
    inverse = lax.rsqrt(jnp.mean(center * center, axis=-1, keepdims=True) + EPSILON)
    normed = center * inverse
    attn_in = (normed * gain_one.astype(f32) + shift_one.astype(f32)).astype(bf16)
    feed_in = (normed * gain_two.astype(f32) + shift_two.astype(f32)).astype(bf16)

    joined_out = jnp.dot(attn_in, joined_matrix, preferred_element_type=f32) + joined_offset.astype(
        f32
    )
    queries = rotate(
        joined_out[:, :own].reshape(total_rows, heads, HEAD), cos_table, sin_table
    ).astype(bf16)
    keys = rotate(
        joined_out[:, own : 2 * own].reshape(total_rows, heads, HEAD), cos_table, sin_table
    ).astype(bf16)
    values = joined_out[:, 2 * own :].astype(bf16).reshape(total_rows, heads, HEAD)
    causal = positions[:, None] >= positions[None, :]
    scores = jnp.einsum("thd,shd->hts", queries, keys, preferred_element_type=f32) * score_scale
    scores = jnp.where(causal[None], scores, -jnp.inf)
    top_score = jnp.max(scores, axis=-1, keepdims=True)
    log_total = top_score + jnp.log(jnp.sum(jnp.exp(scores - top_score), axis=-1, keepdims=True))
    exact_probs = jnp.exp(scores - log_total)
    probs_low = exact_probs.astype(bf16)
    context = (
        jnp.einsum("hts,shd->thd", probs_low, values, preferred_element_type=f32)
        .reshape(total_rows, own)
        .astype(bf16)
    )
    pre_act = jnp.dot(feed_in, up_matrix, preferred_element_type=f32) + up_bias.astype(f32)
    activated = (0.5 * pre_act * (1.0 + lax.erf(pre_act * ROOT_HALF))).astype(bf16)
    branch_part = jnp.dot(context, proj_weight, preferred_element_type=f32) + jnp.dot(
        activated, down_weight, preferred_element_type=f32
    )

    bias_sum = jnp.sum(out_cotangent.astype(f32), axis=0)
    down_grad = jnp.dot(activated.T, cotangent, preferred_element_type=f32)
    pre_grad = jnp.dot(cotangent, down_weight.T, preferred_element_type=f32) * gelu_slope(pre_act)
    pre_low = pre_grad.astype(bf16)
    up_grad = jnp.dot(feed_in.T, pre_low, preferred_element_type=f32)
    up_bgrad = jnp.sum(pre_grad, axis=0)
    feed_in_grad = jnp.dot(pre_low, up_matrix.T, preferred_element_type=f32)
    proj_grad = jnp.dot(context.T, cotangent, preferred_element_type=f32)
    context_grad = (
        jnp.dot(cotangent, proj_weight.T, preferred_element_type=f32)
        .astype(bf16)
        .reshape(total_rows, heads, HEAD)
    )
    row_dots = jnp.sum(
        context_grad.astype(f32) * context.reshape(total_rows, heads, HEAD).astype(f32), axis=-1
    ).T
    probs_grad = jnp.einsum("thd,shd->hts", context_grad, values, preferred_element_type=f32)
    score_grad = (exact_probs * (probs_grad - row_dots[:, :, None]) * score_scale).astype(bf16)
    query_grad = jnp.einsum("hts,shd->thd", score_grad, keys, preferred_element_type=f32)
    key_grad = jnp.einsum("hts,thd->shd", score_grad, queries, preferred_element_type=f32)
    value_grad = jnp.einsum("hts,thd->shd", probs_low, context_grad, preferred_element_type=f32)
    joined_grad = jnp.concatenate(
        [
            rotate_back(query_grad, cos_table, sin_table).reshape(total_rows, own),
            rotate_back(key_grad, cos_table, sin_table).reshape(total_rows, own),
            value_grad.reshape(total_rows, own),
        ],
        axis=1,
    )
    joined_low = joined_grad.astype(bf16)
    qkv_grad = jnp.dot(attn_in.T, joined_low, preferred_element_type=f32)
    qkv_bgrad = jnp.sum(joined_grad, axis=0)
    attn_in_grad = jnp.dot(joined_low, joined_matrix.T, preferred_element_type=f32)

    scaled_part = attn_in_grad * gain_one.astype(f32) + feed_in_grad * gain_two.astype(f32)
    sums = lax.psum_scatter(
        jnp.concatenate(
            [
                branch_part.reshape(group, rows, width),
                scaled_part.reshape(group, rows, width),
            ],
            axis=1,
        ).astype(bf16),
        "cp",
        scatter_dimension=0,
        tiled=False,
    ).astype(f32)
    block_output = (
        block_input.astype(f32)
        + sums[:rows]
        + proj_offset.astype(f32)
        + down_offset.astype(f32)
    ).astype(bf16)
    scaled = sums[rows:]
    own_center = block_input.astype(f32)
    own_center = own_center - jnp.mean(own_center, axis=-1, keepdims=True)
    own_inverse = lax.rsqrt(jnp.mean(own_center * own_center, axis=-1, keepdims=True) + EPSILON)
    own_normed = own_center * own_inverse
    input_grad = out_cotangent.astype(f32) + own_inverse * (
        scaled
        - jnp.mean(scaled, axis=-1, keepdims=True)
        - own_normed * jnp.mean(scaled * own_normed, axis=-1, keepdims=True)
    )

    qkv_bgrad_placed = lax.dynamic_update_slice_in_dim(
        jnp.zeros((3, group, own), f32), qkv_bgrad.reshape(3, 1, own), rank, axis=1
    ).reshape(group, qkv_cols)
    up_bgrad_placed = lax.dynamic_update_slice_in_dim(
        jnp.zeros((group, hidden), f32), up_bgrad[None], rank, axis=0
    )
    vectors = jnp.concatenate(
        [qkv_bgrad_placed, up_bgrad_placed]
        + [
            term.reshape(group, own)
            for term in (
                bias_sum,
                jnp.sum(attn_in_grad * normed, axis=0),
                jnp.sum(attn_in_grad, axis=0),
                jnp.sum(feed_in_grad * normed, axis=0),
                jnp.sum(feed_in_grad, axis=0),
            )
        ],
        axis=1,
    )
    vectors = lax.dynamic_index_in_dim(
        lax.psum(vectors, ("rep", "cp")), rank, 0, keepdims=False
    )
    cuts = [qkv_cols, qkv_cols + hidden] + [
        qkv_cols + hidden + i * own for i in range(1, 5)
    ]
    (qkvb_out, upb_out, bias_out, gain1_out, shift1_out, gain2_out, shift2_out) = jnp.split(
        vectors, cuts
    )

    wide = jnp.concatenate([qkv_grad, up_grad], axis=1).astype(bf16)
    wide = wide.reshape(group, reps, own // reps, part_cols).transpose(1, 0, 2, 3)
    tall = jnp.concatenate([proj_grad, down_grad], axis=0).astype(bf16)
    wide_flat = wide.reshape(reps, -1, width)
    tall_flat = tall.reshape(reps, -1, width)
    both = lax.psum_scatter(
        jnp.concatenate([wide_flat, tall_flat], axis=1), "rep", scatter_dimension=0, tiled=False
    )
    cut = wide_flat.shape[1]
    moved = lax.all_to_all(
        both[:cut].reshape(group, own // reps, part_cols), "cp", 0, 0
    ).reshape(cut, width)
    gathered = lax.all_gather(jnp.concatenate([moved, both[cut:]], axis=0), "rep", axis=0).astype(
        f32
    )
    wide_out = (
        gathered[:, :cut]
        .reshape(reps, group, own // reps, part_cols)
        .transpose(0, 2, 1, 3)
        .reshape(own, group, part_cols)
    )
    qkv_out = (
        wide_out[:, :, :qkv_cols]
        .reshape(own, group, 3, own)
        .transpose(0, 2, 1, 3)
        .reshape(own, group * qkv_cols)
    )
    up_out = wide_out[:, :, qkv_cols:].reshape(own, group * hidden)
    tall_out = gathered[:, cut:].reshape(-1, width)
    return (
        block_output,
        input_grad,
        qkv_out,
        qkvb_out,
        tall_out[:own],
        bias_out,
        up_out,
        upb_out,
        tall_out[own:],
        bias_out,
        gain1_out,
        shift1_out,
        gain2_out,
        shift2_out,
    )


def solution(mesh):
    return jax.shard_map(
        body,
        mesh=mesh,
        in_specs=(
            P(("rep", "cp"), None),
            P("cp", None),
            P("cp"),
            P("cp", None),
            P("cp"),
            P("cp", None),
            P("cp"),
            P("cp", None),
            P("cp"),
            P("cp"),
            P("cp"),
            P("cp"),
            P("cp"),
            P(("rep", "cp"), None),
        ),
        out_specs=(
            P(("rep", "cp"), None),
            P(("rep", "cp"), None),
            P("cp", None),
            P("cp"),
            P("cp", None),
            P("cp"),
            P("cp", None),
            P("cp"),
            P("cp", None),
            P("cp"),
            P("cp"),
            P("cp"),
            P("cp"),
            P("cp"),
        ),
        check_vma=False,
    )
```

```python
import functools

import jax
import jax.numpy as jnp
from jax import lax
from jax.experimental import pallas as pl
from jax.experimental.pallas import tpu as pltpu
from jax.sharding import PartitionSpec as P

HEAD = 64
ROT = 16


EPSILON = 1e-05
ROOT_HALF = 0.7071067811865476
INV_ROOT_TWO_PI = 0.3989422804014327


def layer_norm(inputs, norm_gain, norm_shift):
    center = inputs - jnp.mean(inputs, axis=-1, keepdims=True)
    inverse = lax.rsqrt(jnp.mean(center * center, axis=-1, keepdims=True) + EPSILON)
    normed = center * inverse
    return (
        normed * norm_gain.astype(jnp.float32) + norm_shift.astype(jnp.float32),
        normed,
        inverse,
    )


def norm_back(upstream, normed, inverse, norm_gain):
    scaled = upstream * norm_gain.astype(jnp.float32)
    return inverse * (
        scaled
        - jnp.mean(scaled, axis=-1, keepdims=True)
        - normed * jnp.mean(scaled * normed, axis=-1, keepdims=True)
    )


def rotary_tables(positions):
    half_rot = ROT // 2
    inverse_freq = 1.0 / 10000.0 ** (jnp.arange(half_rot, dtype=jnp.float32) * (2.0 / ROT))
    angles = positions.astype(jnp.float32)[:, None] * inverse_freq[None, :]
    cos_table = jnp.concatenate([jnp.cos(angles), jnp.cos(angles)], axis=-1)
    sin_table = jnp.concatenate([jnp.sin(angles), jnp.sin(angles)], axis=-1)
    return (cos_table, sin_table)


def rotate(heads_in, cos_table, sin_table):
    half_rot = ROT // 2
    rotary_part = heads_in[..., :ROT]
    turned = jnp.concatenate([-rotary_part[..., half_rot:], rotary_part[..., :half_rot]], axis=-1)
    rotated = rotary_part * cos_table[:, None, :] + turned * sin_table[:, None, :]
    return jnp.concatenate([rotated, heads_in[..., ROT:]], axis=-1)


def rotate_back(heads_grad, cos_table, sin_table):
    half_rot = ROT // 2
    sined = heads_grad[..., :ROT] * sin_table[:, None, :]
    swapped = jnp.concatenate([sined[..., half_rot:], -sined[..., :half_rot]], axis=-1)
    rotated = heads_grad[..., :ROT] * cos_table[:, None, :] + swapped
    return jnp.concatenate([rotated, heads_grad[..., ROT:]], axis=-1)


def gelu_slope(preact):
    return (
        0.5 * (1.0 + lax.erf(preact * ROOT_HALF))
        + preact * jnp.exp(-0.5 * preact * preact) * INV_ROOT_TWO_PI
    )

SPLIT = 8
BITS = 3


def rep_bit(r, k):
    return (r // (1 << k)) % 2


def rep_partner(r, k):
    return r + (1 << k) * (1 - 2 * rep_bit(r, k))


def greet(group, reps, z, r, rep_bits):
    barrier = pltpu.get_barrier_semaphore()
    for t in range(1, group):
        pl.semaphore_signal(barrier, inc=1, device_id={"cp": (z + t) % group})
    for k in range(rep_bits):
        pl.semaphore_signal(barrier, inc=1, device_id={"rep": rep_partner(r, k)})
    pl.semaphore_wait(barrier, group - 1 + rep_bits)


def remote(src, dst, send, recv, device):
    return pltpu.make_async_remote_copy(
        src_ref=src, dst_ref=dst, send_sem=send, recv_sem=recv, device_id=device
    )


HALF_BITS = ((1, 2), (2, 1))


def gather_kernel(
    group, reps,
    x_ref, c_ref, s_ref, pu_ref, pq_ref,
    xa_ref, ca_ref, sa_ref, cu_ref, cq_ref,
    loc_sem, line_send, line_recv, small_send, small_recv, z_send, z_recv, g_send, g_recv,
):
    z = lax.axis_index("cp")
    r = lax.axis_index("rep")
    greet(group, reps, z, r, BITS)
    core = rep_bit(r, 0)
    pieces = (pu_ref, pq_ref)
    full = (cu_ref, cq_ref)

    def own(h):
        d1, d2 = HALF_BITS[h]
        return full[h].at[core, rep_bit(r, d1), rep_bit(r, d2)]

    waits = []
    for h in range(2):
        for t in range(1, group):
            to = (z + t) % group
            copy = remote(
                pieces[h].at[to], own(h).at[z], z_send.at[h, t], z_recv.at[h, t], {"cp": to}
            )
            copy.start()
            waits.append(copy)
    for t in range(1, group):
        copy = remote(
            s_ref, sa_ref.at[z], small_send.at[t], small_recv.at[t], {"cp": (z + t) % group}
        )
        copy.start()
        waits.append(copy)
    lines = ((x_ref, xa_ref), (c_ref, ca_ref))

    def line_copy(i, source, direction, first):
        src = lines[i][0] if first else lines[i][1].at[source]
        return remote(
            src,
            lines[i][1].at[source],
            line_send.at[i, direction, source],
            line_recv.at[i, source],
            {"cp": z + 1 - 2 * direction},
        )

    for i in range(2):
        @pl.when(z < group - 1)
        def _():
            line_copy(i, z, 0, True).start()

        @pl.when(z > 0)
        def _():
            line_copy(i, z, 1, True).start()
    locals_ = [
        pltpu.make_async_copy(x_ref, xa_ref.at[z], loc_sem.at[0]),
        pltpu.make_async_copy(c_ref, ca_ref.at[z], loc_sem.at[1]),
        pltpu.make_async_copy(s_ref, sa_ref.at[z], loc_sem.at[2]),
        pltpu.make_async_copy(pu_ref.at[z], own(0).at[z], loc_sem.at[3]),
        pltpu.make_async_copy(pq_ref.at[z], own(1).at[z], loc_sem.at[4]),
    ]
    for copy in locals_:
        copy.start()
    for copy in locals_:
        copy.wait()

    for copy in waits:
        copy.wait()

    def stage_copy(h, stage):
        d1, d2 = HALF_BITS[h]
        if stage == 0:
            ref, bit = own(h), d2
        elif stage == 1:
            ref, bit = full[h].at[core, rep_bit(r, d1)], d1
        else:
            ref, bit = full[h].at[core], 0
        return remote(
            ref, ref, g_send.at[h, stage], g_recv.at[h, stage], {"rep": rep_partner(r, bit)}
        )

    def step(t):
        for i in range(2):
            @pl.when(z >= t)
            def _():
                line_copy(i, z - t, 0, False).wait_recv()

                @pl.when(z < group - 1)
                def _():
                    line_copy(i, z - t, 0, False).start()

            @pl.when(z + t < group)
            def _():
                line_copy(i, z + t, 1, False).wait_recv()

                @pl.when(z > 0)
                def _():
                    line_copy(i, z + t, 1, False).start()

    stages = [[stage_copy(h, s) for h in range(2)] for s in range(BITS)]
    for copy in stages[0]:
        copy.start()
    for s in range(BITS):
        for copy in stages[s]:
            copy.wait()
        if s + 1 < BITS:
            for copy in stages[s + 1]:
                copy.start()
        if s + 1 < group:
            step(s + 1)
    for t in range(BITS + 1, group):
        step(t)
    for i in range(2):
        for t in range(group):
            @pl.when((z >= t) & (z < group - 1))
            def _():
                line_copy(i, z - t, 0, t == 0).wait_send()

            @pl.when((z + t < group) & (z > 0))
            def _():
                line_copy(i, z + t, 1, t == 0).wait_send()


def reduce_kernel(
    group, reps, rep_bits,
    qkv_ref, up_ref, proj_ref, down_ref, vec_ref, parts_ref, x_ref, c_ref, bias_ref,
    y_ref, dx_ref, qkv_out, proj_out, up_out, down_out, vec_out,
    buf_a, buf_b, r0_a, r0_b, r1_a, r1_b, r2_a, r2_b, up_send_a, up_send_b, ru_a, ru_b,
    zr_a, zr_b, full_a, full_b, vs, vr, vz, sr,
    rs_send, rs_recv, u_send, u_recv, z_send, z_recv, g_send, g_recv,
    v_send, v_recv, vz_send, vz_recv, s_send, s_recv,
):
    f32, bf16 = jnp.float32, jnp.bfloat16
    z = lax.axis_index("cp")
    r = lax.axis_index("rep")
    greet(group, reps, z, r, rep_bits)
    core = rep_bit(r, 0)
    rows = x_ref.shape[0]
    own, width = proj_ref.shape
    unit = own // SPLIT
    hidden = up_ref.shape[1]
    qkv_cols = qkv_ref.shape[1]
    half_w = buf_a.shape[-1]
    cut = half_w - hidden
    buf = (buf_a, buf_b)
    r0 = (r0_a, r0_b)
    r1 = (r1_a, r1_b)
    r2 = (r2_a, r2_b)
    up_send = (up_send_a, up_send_b)
    ru = (ru_a, ru_b)
    zr = (zr_a, zr_b)
    full = (full_a, full_b)
    zw = (zr_a.shape[-1], zr_b.shape[-1])

    sums = []
    for t in range(1, group):
        to = (z + t) % group
        copy = remote(parts_ref.at[to], sr.at[t - 1], s_send.at[t], s_recv.at[t], {"cp": to})
        sums.append(copy)

    def fill(s, core_bit):
        first, second = s // 2, s % 2
        base = (core_bit * 4 + s) * unit
        proj = proj_ref[pl.ds(pl.multiple_of(base, 8), unit), :].astype(bf16)
        for u in range(group):
            at = pl.ds(pl.multiple_of(u * own + base, 8), unit)
            down = down_ref[at, :].astype(bf16)
            buf_a[core_bit, first, second, u] = jnp.concatenate(
                [up_ref[at, :].astype(bf16), down[:, :cut]], axis=1
            )
            buf_b[core_bit, second, first, u] = jnp.concatenate(
                [
                    qkv_ref[at, :].astype(bf16),
                    proj[:, u * (width // group) : (u + 1) * (width // group)],
                    down[:, cut:],
                ],
                axis=1,
            )

    def fill_loop(core_bit):
        lax.fori_loop(0, 4, lambda s, n: (fill(s, core_bit), n)[1], 0)

    def rs_copy(h, stage):
        d1, d2 = HALF_BITS[h]
        if stage == 0:
            src, dst, bit = buf[h].at[1 - core], r0[h], 0
        elif stage == 1:
            src, dst, bit = r0[h].at[1 - rep_bit(r, d1)], r1[h], d1
        else:
            src, dst, bit = r1[h].at[1 - rep_bit(r, d2)], r2[h], d2
        return remote(
            src, dst, rs_send.at[h, stage], rs_recv.at[h, stage], {"rep": rep_partner(r, bit)}
        )

    def v_copy(k):
        return remote(
            vs.at[k], vr.at[k], v_send.at[k], v_recv.at[k], {"rep": rep_partner(r, k)}
        )

    fill_loop(1 - core)
    rs = [[rs_copy(h, s) for h in range(2)] for s in range(BITS)]
    for copy in rs[0]:
        copy.start()
    vs[0] = vec_ref[...]
    v_copy(0).start()
    for copy in sums:
        copy.start()
    fill_loop(core)

    for h in range(2):
        rs[0][h].wait()

        def add0(n, carry):
            a, b, u = n // (2 * group), (n // group) % 2, n % group
            r0[h][a, b, u] = (
                r0[h][a, b, u].astype(f32) + buf[h][core, a, b, u].astype(f32)
            ).astype(bf16)
            return carry

        lax.fori_loop(0, 4 * group, add0, 0)
        rs[1][h].start()
    v_copy(0).wait()
    vs[1] = vs[0] + vr[0]
    v_copy(1).start()
    for h in range(2):
        rs[1][h].wait()
        mine = rep_bit(r, HALF_BITS[h][0])

        def add1(n, carry):
            b, u = n // group, n % group
            r1[h][b, u] = (
                r1[h][b, u].astype(f32) + r0[h][mine, b, u].astype(f32)
            ).astype(bf16)
            return carry

        lax.fori_loop(0, 2 * group, add1, 0)
        rs[2][h].start()
    v_copy(1).wait()
    vs[2] = vs[1] + vr[1]
    v_copy(2).start()
    for h in range(2):
        rs[2][h].wait()
        mine = rep_bit(r, HALF_BITS[h][1])
        for u in range(group):
            up_send[h][0, u] = (
                r2[h][u].astype(f32) + r1[h][mine, u].astype(f32)
            ).astype(bf16)
    v_copy(2).wait()
    vs[3] = vs[2] + vr[2]
    for k in range(BITS, rep_bits):
        copies = [
            remote(
                up_send[h].at[k - BITS],
                ru[h].at[k - BITS],
                u_send.at[h, k - BITS],
                u_recv.at[h, k - BITS],
                {"rep": rep_partner(r, k)},
            )
            for h in range(2)
        ] + [v_copy(k)]
        for copy in copies:
            copy.start()
        for copy in copies:
            copy.wait()
        for h in range(2):
            up_send[h][k - BITS + 1] = (
                up_send[h][k - BITS].astype(f32) + ru[h][k - BITS].astype(f32)
            ).astype(bf16)
        vs[k + 1] = vs[k] + vr[k]
    last = rep_bits - BITS
    final = [up_send[h].at[last] for h in range(2)]
    exchange = []
    for t in range(1, group):
        to = (z + t) % group
        for h in range(2):
            exchange.append(
                remote(
                    final[h].at[to, :, pl.ds(0, zw[h])],
                    zr[h].at[t - 1],
                    z_send.at[h, t],
                    z_recv.at[h, t],
                    {"cp": to},
                )
            )
        exchange.append(
            remote(
                vs.at[rep_bits, to], vz.at[t - 1], vz_send.at[t], vz_recv.at[t], {"cp": to}
            )
        )
    for copy in exchange:
        copy.start()

    def mine_of(h):
        d1, d2 = HALF_BITS[h]
        return full[h].at[core, rep_bit(r, d1), rep_bit(r, d2)]

    for copy in exchange:
        copy.wait()
    used = (hidden, qkv_cols)
    for h in range(2):
        piece = mine_of(h)
        for u in range(group):
            piece[u, :, used[h] :] = final[h][u, :, used[h] :]
        piece[z, :, : used[h]] = final[h][z, :, : used[h]]
        for t in range(1, group):
            piece[(z + group - t) % group, :, : used[h]] = zr[h][t - 1][:, : used[h]]
    total = vs[rep_bits, z]
    for t in range(1, group):
        total = total + vz[t - 1]
    vec_out[...] = total

    def g_copy(h, stage):
        d1, d2 = HALF_BITS[h]
        if stage == 0:
            ref, bit = mine_of(h), d2
        elif stage == 1:
            ref, bit = full[h].at[core, rep_bit(r, d1)], d1
        else:
            ref, bit = full[h].at[core], 0
        return remote(
            ref, ref, g_send.at[h, stage], g_recv.at[h, stage], {"rep": rep_partner(r, bit)}
        )

    gather = [[g_copy(h, s) for h in range(2)] for s in range(BITS)]
    for copy in gather[0]:
        copy.start()
    for copy in sums:
        copy.wait()
    xs = x_ref[...].astype(f32)
    branch = xs + bias_ref[...]
    scaled = parts_ref[z, rows:].astype(f32)
    branch = branch + parts_ref[z, :rows].astype(f32)
    for t in range(1, group):
        branch = branch + sr[t - 1, :rows].astype(f32)
        scaled = scaled + sr[t - 1, rows:].astype(f32)
    y_ref[...] = branch.astype(bf16)
    center = xs - jnp.mean(xs, axis=-1, keepdims=True)
    inverse = lax.rsqrt(jnp.mean(center * center, axis=-1, keepdims=True) + EPSILON)
    normed = center * inverse
    dx_ref[...] = c_ref[...].astype(f32) + inverse * (
        scaled
        - jnp.mean(scaled, axis=-1, keepdims=True)
        - normed * jnp.mean(scaled * normed, axis=-1, keepdims=True)
    )
    for s in range(BITS):
        for h in range(2):
            gather[s][h].wait()
            if s + 1 < BITS:
                gather[s + 1][h].start()

    def write(s, carry):
        c0, first, second = s // 4, (s // 2) % 2, s % 2
        base = s * unit
        at = pl.ds(pl.multiple_of(base, 8), unit)
        for u in range(group):
            a = full_a[c0, first, second, u].astype(f32)
            b = full_b[c0, second, first, u].astype(f32)
            up_out[at, u * hidden : (u + 1) * hidden] = a[:, :hidden]
            rows_at = pl.ds(pl.multiple_of(u * own + base, 8), unit)
            down_out[rows_at, :cut] = a[:, hidden:]
            down_out[rows_at, cut:] = b[:, qkv_cols + width // group :]
            proj_out[at, u * (width // group) : (u + 1) * (width // group)] = b[
                :, qkv_cols : qkv_cols + width // group
            ]
            for j in range(3):
                qkv_out[at, j * width + u * own : j * width + (u + 1) * own] = b[
                    :, j * own : (j + 1) * own
                ]
        return carry

    lax.fori_loop(0, SPLIT, write, 0)


def body(
    block_input,
    qkv_weight,
    qkv_bias,
    proj_weight,
    proj_bias,
    up_weight,
    up_bias,
    down_weight,
    down_bias,
    attention_gain,
    attention_shift,
    feed_gain,
    feed_shift,
    out_cotangent,
):
    f32, bf16 = jnp.float32, jnp.bfloat16
    group = lax.axis_size("cp")
    reps = lax.axis_size("rep")
    rank = lax.axis_index("cp")
    rows, width = block_input.shape
    own = width // group
    heads = own // HEAD
    total_rows = rows * group
    hidden = up_weight.shape[1] // group
    qkv_cols = 3 * own
    part_cols = qkv_cols + hidden
    score_scale = HEAD ** (-0.5)

    small = jnp.concatenate(
        [qkv_bias, proj_bias, down_bias, attention_gain, attention_shift, feed_gain, feed_shift]
    )
    small = jnp.pad(small, (0, -small.shape[0] % 128))[None]
    unit = own // SPLIT
    r = lax.axis_index("rep")
    slot = rep_bit(r, 0) * 4 + rep_bit(r, 1) * 2 + rep_bit(r, 2)
    up_piece = (
        lax.dynamic_slice_in_dim(up_weight, slot * unit, unit, axis=0)
        .reshape(unit, group, hidden)
        .transpose(1, 0, 2)
    )
    qkv_piece = (
        lax.dynamic_slice_in_dim(qkv_weight, slot * unit, unit, axis=0)
        .reshape(unit, 3, group, own)
        .transpose(2, 0, 1, 3)
        .reshape(group, unit, qkv_cols)
    )
    vmem = pl.BlockSpec(memory_space=pltpu.VMEM)
    dma = pltpu.SemaphoreType.DMA
    tokens, cotangent, small_all, up_slices, qkv_slices = pl.pallas_call(
        functools.partial(gather_kernel, group, reps),
        out_shape=[
            jax.ShapeDtypeStruct((group, rows, width), bf16),
            jax.ShapeDtypeStruct((group, rows, width), bf16),
            jax.ShapeDtypeStruct((group,) + small.shape, bf16),
            jax.ShapeDtypeStruct((2, 2, 2) + up_piece.shape, bf16),
            jax.ShapeDtypeStruct((2, 2, 2) + qkv_piece.shape, bf16),
        ],
        in_specs=[vmem] * 5,
        out_specs=[vmem] * 5,
        scratch_shapes=[
            dma((5,)),
            dma((2, 2, group)),
            dma((2, group)),
            dma((group,)),
            dma((group,)),
            dma((2, group)),
            dma((2, group)),
            dma((2, BITS)),
            dma((2, BITS)),
        ],
        compiler_params=pltpu.CompilerParams(
            collective_id=0, has_side_effects=True, vmem_limit_bytes=50 * 2**20
        ),
    )(block_input, out_cotangent, small, up_piece, qkv_piece)
    tokens = tokens.reshape(total_rows, width)
    cotangent = cotangent.reshape(total_rows, width)
    small_all = small_all.reshape(group, -1)
    joined_offset_all = small_all[:, :qkv_cols].reshape(group * qkv_cols)
    joined_offset = lax.dynamic_slice_in_dim(
        joined_offset_all.reshape(3, group, own), rank, 1, axis=1
    ).reshape(qkv_cols)
    proj_offset, down_offset, gain_one, shift_one, gain_two, shift_two = (
        small_all[:, qkv_cols + i * own : qkv_cols + (i + 1) * own].reshape(width)
        for i in range(6)
    )

    up_matrix = up_slices.transpose(3, 0, 1, 2, 4, 5).reshape(width, hidden)
    joined_matrix = qkv_slices.transpose(3, 0, 2, 1, 4, 5).reshape(width, qkv_cols)

    positions = jnp.arange(total_rows, dtype=jnp.int32)
    cos_table, sin_table = rotary_tables(positions)
    widened = tokens.astype(f32)
    center = widened - jnp.mean(widened, axis=-1, keepdims=True)
    inverse = lax.rsqrt(jnp.mean(center * center, axis=-1, keepdims=True) + EPSILON)
    normed = center * inverse
    attn_in = (normed * gain_one.astype(f32) + shift_one.astype(f32)).astype(bf16)
    feed_in = (normed * gain_two.astype(f32) + shift_two.astype(f32)).astype(bf16)

    joined_out = jnp.dot(attn_in, joined_matrix, preferred_element_type=f32) + joined_offset.astype(
        f32
    )
    queries = rotate(
        joined_out[:, :own].reshape(total_rows, heads, HEAD), cos_table, sin_table
    ).astype(bf16)
    keys = rotate(
        joined_out[:, own : 2 * own].reshape(total_rows, heads, HEAD), cos_table, sin_table
    ).astype(bf16)
    values = joined_out[:, 2 * own :].astype(bf16).reshape(total_rows, heads, HEAD)
    causal = positions[:, None] >= positions[None, :]
    scores = jnp.einsum("thd,shd->hts", queries, keys, preferred_element_type=f32) * score_scale
    scores = jnp.where(causal[None], scores, -jnp.inf)
    top_score = jnp.max(scores, axis=-1, keepdims=True)
    log_total = top_score + jnp.log(jnp.sum(jnp.exp(scores - top_score), axis=-1, keepdims=True))
    exact_probs = jnp.exp(scores - log_total)
    probs_low = exact_probs.astype(bf16)
    context = (
        jnp.einsum("hts,shd->thd", probs_low, values, preferred_element_type=f32)
        .reshape(total_rows, own)
        .astype(bf16)
    )
    pre_act = jnp.dot(feed_in, up_matrix, preferred_element_type=f32) + up_bias.astype(f32)
    activated = (0.5 * pre_act * (1.0 + lax.erf(pre_act * ROOT_HALF))).astype(bf16)
    branch_part = jnp.dot(context, proj_weight, preferred_element_type=f32) + jnp.dot(
        activated, down_weight, preferred_element_type=f32
    )

    bias_sum = jnp.sum(out_cotangent.astype(f32), axis=0)
    down_grad = jnp.dot(activated.T, cotangent, preferred_element_type=f32)
    pre_grad = jnp.dot(cotangent, down_weight.T, preferred_element_type=f32) * gelu_slope(pre_act)
    pre_low = pre_grad.astype(bf16)
    up_grad = jnp.dot(feed_in.T, pre_low, preferred_element_type=f32)
    up_bgrad = jnp.sum(pre_grad, axis=0)
    feed_in_grad = jnp.dot(pre_low, up_matrix.T, preferred_element_type=f32)
    proj_grad = jnp.dot(context.T, cotangent, preferred_element_type=f32)
    context_grad = (
        jnp.dot(cotangent, proj_weight.T, preferred_element_type=f32)
        .astype(bf16)
        .reshape(total_rows, heads, HEAD)
    )
    row_dots = jnp.sum(
        context_grad.astype(f32) * context.reshape(total_rows, heads, HEAD).astype(f32), axis=-1
    ).T
    probs_grad = jnp.einsum("thd,shd->hts", context_grad, values, preferred_element_type=f32)
    score_grad = (exact_probs * (probs_grad - row_dots[:, :, None]) * score_scale).astype(bf16)
    query_grad = jnp.einsum("hts,shd->thd", score_grad, keys, preferred_element_type=f32)
    key_grad = jnp.einsum("hts,thd->shd", score_grad, queries, preferred_element_type=f32)
    value_grad = jnp.einsum("hts,thd->shd", probs_low, context_grad, preferred_element_type=f32)
    joined_grad = jnp.concatenate(
        [
            rotate_back(query_grad, cos_table, sin_table).reshape(total_rows, own),
            rotate_back(key_grad, cos_table, sin_table).reshape(total_rows, own),
            value_grad.reshape(total_rows, own),
        ],
        axis=1,
    )
    joined_low = joined_grad.astype(bf16)
    qkv_grad = jnp.dot(attn_in.T, joined_low, preferred_element_type=f32)
    qkv_bgrad = jnp.sum(joined_grad, axis=0)
    attn_in_grad = jnp.dot(joined_low, joined_matrix.T, preferred_element_type=f32)

    scaled_part = attn_in_grad * gain_one.astype(f32) + feed_in_grad * gain_two.astype(f32)
    parts = jnp.concatenate(
        [branch_part.reshape(group, rows, width), scaled_part.reshape(group, rows, width)], axis=1
    ).astype(bf16)
    bias_row = (proj_offset.astype(f32) + down_offset.astype(f32))[None]

    qkv_bgrad_placed = lax.dynamic_update_slice_in_dim(
        jnp.zeros((3, group, own), f32), qkv_bgrad.reshape(3, 1, own), rank, axis=1
    ).reshape(group, qkv_cols)
    up_bgrad_placed = lax.dynamic_update_slice_in_dim(
        jnp.zeros((group, hidden), f32), up_bgrad[None], rank, axis=0
    )
    vectors = jnp.concatenate(
        [qkv_bgrad_placed, up_bgrad_placed]
        + [
            term.reshape(group, own)
            for term in (
                bias_sum,
                jnp.sum(attn_in_grad * normed, axis=0),
                jnp.sum(attn_in_grad, axis=0),
                jnp.sum(feed_in_grad * normed, axis=0),
                jnp.sum(feed_in_grad, axis=0),
            )
        ],
        axis=1,
    )
    rep_bits = reps.bit_length() - 1
    half_w = (qkv_cols + own + width + hidden) // 2
    piece = (group, unit, half_w)
    halves = lambda *lead: [pltpu.VMEM(lead + piece, bf16)] * 2
    spare = max(rep_bits - BITS, 1)
    (block_output, input_grad, qkv_out, proj_out, up_out, down_out, vectors) = pl.pallas_call(
        functools.partial(reduce_kernel, group, reps, rep_bits),
        out_shape=[
            jax.ShapeDtypeStruct((rows, width), bf16),
            jax.ShapeDtypeStruct((rows, width), f32),
            jax.ShapeDtypeStruct((own, group * qkv_cols), f32),
            jax.ShapeDtypeStruct((own, width), f32),
            jax.ShapeDtypeStruct((own, group * hidden), f32),
            jax.ShapeDtypeStruct((hidden, width), f32),
            jax.ShapeDtypeStruct((1, vectors.shape[1]), f32),
        ],
        in_specs=[vmem] * 9,
        out_specs=[vmem] * 7,
        scratch_shapes=(
            halves(2, 2, 2)
            + halves(2, 2)
            + halves(2)
            + halves()
            + halves(rep_bits - BITS + 1)
            + halves(spare)
            + [
                pltpu.VMEM((group - 1, unit, hidden), bf16),
                pltpu.VMEM((group - 1, unit, -(-qkv_cols // 128) * 128), bf16),
            ]
            + halves(2, 2, 2)
            + [
                pltpu.VMEM((rep_bits + 1, group, 1, vectors.shape[1]), f32),
                pltpu.VMEM((rep_bits, group, 1, vectors.shape[1]), f32),
                pltpu.VMEM((group - 1, 1, vectors.shape[1]), f32),
                pltpu.VMEM((group - 1, 2 * rows, width), bf16),
                dma((2, BITS)),
                dma((2, BITS)),
                dma((2, spare)),
                dma((2, spare)),
                dma((2, group)),
                dma((2, group)),
                dma((2, BITS)),
                dma((2, BITS)),
                dma((rep_bits,)),
                dma((rep_bits,)),
                dma((group,)),
                dma((group,)),
                dma((group,)),
                dma((group,)),
            ]
        ),
        compiler_params=pltpu.CompilerParams(
            collective_id=1, has_side_effects=True, vmem_limit_bytes=60 * 2**20
        ),
    )(
        qkv_grad,
        up_grad,
        proj_grad,
        down_grad,
        vectors[:, None],
        parts,
        block_input,
        out_cotangent,
        bias_row,
    )
    vectors = vectors[0]
    cuts = [qkv_cols, qkv_cols + hidden] + [
        qkv_cols + hidden + i * own for i in range(1, 5)
    ]
    (qkvb_out, upb_out, bias_out, gain1_out, shift1_out, gain2_out, shift2_out) = jnp.split(
        vectors, cuts
    )

    return (
        block_output,
        input_grad,
        qkv_out,
        qkvb_out,
        proj_out,
        bias_out,
        up_out,
        upb_out,
        down_out,
        bias_out,
        gain1_out,
        shift1_out,
        gain2_out,
        shift2_out,
    )


def solution(mesh):
    return jax.shard_map(
        body,
        mesh=mesh,
        in_specs=(
            P(("rep", "cp"), None),
            P("cp", None),
            P("cp"),
            P("cp", None),
            P("cp"),
            P("cp", None),
            P("cp"),
            P("cp", None),
            P("cp"),
            P("cp"),
            P("cp"),
            P("cp"),
            P("cp"),
            P(("rep", "cp"), None),
        ),
        out_specs=(
            P(("rep", "cp"), None),
            P(("rep", "cp"), None),
            P("cp", None),
            P("cp"),
            P("cp", None),
            P("cp"),
            P("cp", None),
            P("cp"),
            P("cp", None),
            P("cp"),
            P("cp"),
            P("cp"),
            P("cp"),
            P("cp"),
        ),
        check_vma=False,
    )
```

```python
import functools

import jax
import jax.numpy as jnp
from jax import lax
from jax.experimental import pallas as pl
from jax.experimental.pallas import tpu as pltpu
from jax.sharding import PartitionSpec as P

HEAD = 64
ROT = 16


EPSILON = 1e-05
ROOT_HALF = 0.7071067811865476
INV_ROOT_TWO_PI = 0.3989422804014327


def layer_norm(inputs, norm_gain, norm_shift):
    center = inputs - jnp.mean(inputs, axis=-1, keepdims=True)
    inverse = lax.rsqrt(jnp.mean(center * center, axis=-1, keepdims=True) + EPSILON)
    normed = center * inverse
    return (
        normed * norm_gain.astype(jnp.float32) + norm_shift.astype(jnp.float32),
        normed,
        inverse,
    )


def norm_back(upstream, normed, inverse, norm_gain):
    scaled = upstream * norm_gain.astype(jnp.float32)
    return inverse * (
        scaled
        - jnp.mean(scaled, axis=-1, keepdims=True)
        - normed * jnp.mean(scaled * normed, axis=-1, keepdims=True)
    )


def rotary_tables(positions):
    half_rot = ROT // 2
    inverse_freq = 1.0 / 10000.0 ** (jnp.arange(half_rot, dtype=jnp.float32) * (2.0 / ROT))
    angles = positions.astype(jnp.float32)[:, None] * inverse_freq[None, :]
    cos_table = jnp.concatenate([jnp.cos(angles), jnp.cos(angles)], axis=-1)
    sin_table = jnp.concatenate([jnp.sin(angles), jnp.sin(angles)], axis=-1)
    return (cos_table, sin_table)


def rotate(heads_in, cos_table, sin_table):
    half_rot = ROT // 2
    rotary_part = heads_in[..., :ROT]
    turned = jnp.concatenate([-rotary_part[..., half_rot:], rotary_part[..., :half_rot]], axis=-1)
    rotated = rotary_part * cos_table[:, None, :] + turned * sin_table[:, None, :]
    return jnp.concatenate([rotated, heads_in[..., ROT:]], axis=-1)


def rotate_back(heads_grad, cos_table, sin_table):
    half_rot = ROT // 2
    sined = heads_grad[..., :ROT] * sin_table[:, None, :]
    swapped = jnp.concatenate([sined[..., half_rot:], -sined[..., :half_rot]], axis=-1)
    rotated = heads_grad[..., :ROT] * cos_table[:, None, :] + swapped
    return jnp.concatenate([rotated, heads_grad[..., ROT:]], axis=-1)


def gelu_slope(preact):
    return (
        0.5 * (1.0 + lax.erf(preact * ROOT_HALF))
        + preact * jnp.exp(-0.5 * preact * preact) * INV_ROOT_TWO_PI
    )

SPLIT = 8
BITS = 3


def rep_bit(r, k):
    return (r // (1 << k)) % 2


def rep_partner(r, k):
    return r + (1 << k) * (1 - 2 * rep_bit(r, k))


def greet(group, reps, z, r, rep_bits):
    barrier = pltpu.get_barrier_semaphore()
    for t in range(1, group):
        pl.semaphore_signal(barrier, inc=1, device_id={"cp": (z + t) % group})
    for k in range(rep_bits):
        pl.semaphore_signal(barrier, inc=1, device_id={"rep": rep_partner(r, k)})
    pl.semaphore_wait(barrier, group - 1 + rep_bits)


def remote(src, dst, send, recv, device):
    return pltpu.make_async_remote_copy(
        src_ref=src, dst_ref=dst, send_sem=send, recv_sem=recv, device_id=device
    )


HALF_BITS = ((1, 2), (2, 1))


def gather_kernel(
    group, reps,
    x_ref, c_ref, s_ref, pu_ref, pq_ref,
    xa_ref, ca_ref, sa_ref, cu_ref, cq_ref,
    loc_sem, line_send, line_recv, small_send, small_recv, z_send, z_recv, g_send, g_recv,
):
    z = lax.axis_index("cp")
    r = lax.axis_index("rep")
    greet(group, reps, z, r, BITS)
    core = rep_bit(r, 0)
    pieces = (pu_ref, pq_ref)
    full = (cu_ref, cq_ref)

    def own(h):
        d1, d2 = HALF_BITS[h]
        return full[h].at[core, rep_bit(r, d1), rep_bit(r, d2)]

    waits = []
    for h in range(2):
        for t in range(1, group):
            to = (z + t) % group
            copy = remote(
                pieces[h].at[to], own(h).at[z], z_send.at[h, t], z_recv.at[h, t], {"cp": to}
            )
            copy.start()
            waits.append(copy)
    for t in range(1, group):
        copy = remote(
            s_ref, sa_ref.at[z], small_send.at[t], small_recv.at[t], {"cp": (z + t) % group}
        )
        copy.start()
        waits.append(copy)
    lines = ((x_ref, xa_ref), (c_ref, ca_ref))

    def line_copy(i, source, direction, first):
        src = lines[i][0] if first else lines[i][1].at[source]
        return remote(
            src,
            lines[i][1].at[source],
            line_send.at[i, direction, source],
            line_recv.at[i, source],
            {"cp": z + 1 - 2 * direction},
        )

    for i in range(2):
        @pl.when(z < group - 1)
        def _():
            line_copy(i, z, 0, True).start()

        @pl.when(z > 0)
        def _():
            line_copy(i, z, 1, True).start()
    locals_ = [
        pltpu.make_async_copy(x_ref, xa_ref.at[z], loc_sem.at[0]),
        pltpu.make_async_copy(c_ref, ca_ref.at[z], loc_sem.at[1]),
        pltpu.make_async_copy(s_ref, sa_ref.at[z], loc_sem.at[2]),
        pltpu.make_async_copy(pu_ref.at[z], own(0).at[z], loc_sem.at[3]),
        pltpu.make_async_copy(pq_ref.at[z], own(1).at[z], loc_sem.at[4]),
    ]
    for copy in locals_:
        copy.start()
    for copy in locals_:
        copy.wait()

    for copy in waits:
        copy.wait()

    def stage_copy(h, stage):
        d1, d2 = HALF_BITS[h]
        if stage == 0:
            ref, bit = own(h), d2
        elif stage == 1:
            ref, bit = full[h].at[core, rep_bit(r, d1)], d1
        else:
            ref, bit = full[h].at[core], 0
        return remote(
            ref, ref, g_send.at[h, stage], g_recv.at[h, stage], {"rep": rep_partner(r, bit)}
        )

    def step(t):
        for i in range(2):
            @pl.when(z >= t)
            def _():
                line_copy(i, z - t, 0, False).wait_recv()

                @pl.when(z < group - 1)
                def _():
                    line_copy(i, z - t, 0, False).start()

            @pl.when(z + t < group)
            def _():
                line_copy(i, z + t, 1, False).wait_recv()

                @pl.when(z > 0)
                def _():
                    line_copy(i, z + t, 1, False).start()

    stages = [[stage_copy(h, s) for h in range(2)] for s in range(BITS)]
    for copy in stages[0]:
        copy.start()
    for s in range(BITS):
        for copy in stages[s]:
            copy.wait()
        if s + 1 < BITS:
            for copy in stages[s + 1]:
                copy.start()
        if s + 1 < group:
            step(s + 1)
    for t in range(BITS + 1, group):
        step(t)
    for i in range(2):
        for t in range(group):
            @pl.when((z >= t) & (z < group - 1))
            def _():
                line_copy(i, z - t, 0, t == 0).wait_send()

            @pl.when((z + t < group) & (z > 0))
            def _():
                line_copy(i, z + t, 1, t == 0).wait_send()


def reduce_kernel(
    group, reps, rep_bits,
    qkv_ref, up_ref, proj_ref, down_ref, sum_refs, parts_ref,
    full_a, full_b, sr, vec_out, qkvb_out,
    buf_a, buf_b, r0_a, r0_b, r1_a, r1_b, r2_a, r2_b, up_send_a, up_send_b, ru_a, ru_b,
    zr_a, zr_b, vs, vr, vz,
    rs_send, rs_recv, u_send, u_recv, z_send, z_recv, g_send, g_recv,
    v_send, v_recv, vz_send, vz_recv, s_send, s_recv,
):
    f32, bf16 = jnp.float32, jnp.bfloat16
    z = lax.axis_index("cp")
    r = lax.axis_index("rep")
    greet(group, reps, z, r, rep_bits)
    core = rep_bit(r, 0)
    rows = parts_ref.shape[1] // 2
    own, width = proj_ref.shape
    unit = own // SPLIT
    hidden = up_ref.shape[1]
    qkv_cols = qkv_ref.shape[1]
    half_w = buf_a.shape[-1]
    cut = half_w - hidden
    buf = (buf_a, buf_b)
    r0 = (r0_a, r0_b)
    r1 = (r1_a, r1_b)
    r2 = (r2_a, r2_b)
    up_send = (up_send_a, up_send_b)
    ru = (ru_a, ru_b)
    zr = (zr_a, zr_b)
    full = (full_a, full_b)
    zw = (zr_a.shape[-1], zr_b.shape[-1])

    sums = []
    for i in range(2):
        for t in range(1, group):
            to = (z + t) % group
            at = pl.ds(i * rows, rows)
            sums.append(
                remote(
                    parts_ref.at[to, at],
                    sr.at[t - 1, at],
                    s_send.at[i, t],
                    s_recv.at[i, t],
                    {"cp": to},
                )
            )

    def fill(s, core_bit):
        first, second = s // 2, s % 2
        base = (core_bit * 4 + s) * unit
        proj = proj_ref[pl.ds(pl.multiple_of(base, 8), unit), :].astype(bf16)
        for u in range(group):
            at = pl.ds(pl.multiple_of(u * own + base, 8), unit)
            down = down_ref[at, :].astype(bf16)
            buf_a[core_bit, first, second, u] = jnp.concatenate(
                [up_ref[at, :].astype(bf16), down[:, :cut]], axis=1
            )
            buf_b[core_bit, second, first, u] = jnp.concatenate(
                [
                    qkv_ref[at, :].astype(bf16),
                    proj[:, u * (width // group) : (u + 1) * (width // group)],
                    down[:, cut:],
                ],
                axis=1,
            )

    def fill_loop(core_bit):
        lax.fori_loop(0, 4, lambda s, n: (fill(s, core_bit), n)[1], 0)

    def rs_copy(h, stage):
        d1, d2 = HALF_BITS[h]
        if stage == 0:
            src, dst, bit = buf[h].at[1 - core], r0[h], 0
        elif stage == 1:
            src, dst, bit = r0[h].at[1 - rep_bit(r, d1)], r1[h], d1
        else:
            src, dst, bit = r1[h].at[1 - rep_bit(r, d2)], r2[h], d2
        return remote(
            src, dst, rs_send.at[h, stage], rs_recv.at[h, stage], {"rep": rep_partner(r, bit)}
        )

    def v_copy(k):
        return remote(
            vs.at[k], vr.at[k], v_send.at[k], v_recv.at[k], {"rep": rep_partner(r, k)}
        )

    for copy in sums[: group - 1]:
        copy.start()
    fill_loop(1 - core)
    rs = [[rs_copy(h, s) for h in range(2)] for s in range(BITS)]
    for copy in rs[0]:
        copy.start()
    vs[0] = jnp.zeros(vs.shape[1:], f32)
    for i, ref in enumerate(sum_refs):
        vs[0, i : i + 1, : ref.shape[1]] = ref[...]
    v_copy(0).start()
    fill_loop(core)

    for h in range(2):
        rs[0][h].wait()

        def add0(n, carry):
            a, b, u = n // (2 * group), (n // group) % 2, n % group
            r0[h][a, b, u] = (
                r0[h][a, b, u].astype(f32) + buf[h][core, a, b, u].astype(f32)
            ).astype(bf16)
            return carry

        lax.fori_loop(0, 4 * group, add0, 0)
        rs[1][h].start()
    v_copy(0).wait()
    vs[1] = vs[0] + vr[0]
    v_copy(1).start()
    for h in range(2):
        rs[1][h].wait()
        mine = rep_bit(r, HALF_BITS[h][0])

        def add1(n, carry):
            b, u = n // group, n % group
            r1[h][b, u] = (
                r1[h][b, u].astype(f32) + r0[h][mine, b, u].astype(f32)
            ).astype(bf16)
            return carry

        lax.fori_loop(0, 2 * group, add1, 0)
        rs[2][h].start()
    v_copy(1).wait()
    vs[2] = vs[1] + vr[1]
    v_copy(2).start()
    for h in range(2):
        rs[2][h].wait()
        mine = rep_bit(r, HALF_BITS[h][1])
        for u in range(group):
            up_send[h][0, u] = (
                r2[h][u].astype(f32) + r1[h][mine, u].astype(f32)
            ).astype(bf16)
    v_copy(2).wait()
    vs[3] = vs[2] + vr[2]
    for k in range(BITS, rep_bits):
        copies = [
            remote(
                up_send[h].at[k - BITS],
                ru[h].at[k - BITS],
                u_send.at[h, k - BITS],
                u_recv.at[h, k - BITS],
                {"rep": rep_partner(r, k)},
            )
            for h in range(2)
        ] + [v_copy(k)]
        for copy in copies:
            copy.start()
        for copy in copies:
            copy.wait()
        for h in range(2):
            up_send[h][k - BITS + 1] = (
                up_send[h][k - BITS].astype(f32) + ru[h][k - BITS].astype(f32)
            ).astype(bf16)
        vs[k + 1] = vs[k] + vr[k]
    last = rep_bits - BITS
    final = [up_send[h].at[last] for h in range(2)]
    exchange = []
    for t in range(1, group):
        to = (z + t) % group
        for h in range(2):
            exchange.append(
                remote(
                    final[h].at[to, :, pl.ds(0, zw[h])],
                    zr[h].at[t - 1],
                    z_send.at[h, t],
                    z_recv.at[h, t],
                    {"cp": to},
                )
            )
        exchange.append(
            remote(
                vs.at[rep_bits], vz.at[t - 1], vz_send.at[t], vz_recv.at[t], {"cp": to}
            )
        )
    for copy in exchange:
        copy.start()
    for copy in sums[group - 1 :]:
        copy.start()

    def mine_of(h):
        d1, d2 = HALF_BITS[h]
        return full[h].at[core, rep_bit(r, d1), rep_bit(r, d2)]

    for copy in exchange:
        copy.wait()
    used = (hidden, qkv_cols)
    for h in range(2):
        piece = mine_of(h)
        for u in range(group):
            piece[u, :, used[h] :] = final[h][u, :, used[h] :]
        piece[z, :, : used[h]] = final[h][z, :, : used[h]]
        for t in range(1, group):
            piece[(z + group - t) % group, :, : used[h]] = zr[h][t - 1][:, : used[h]]
    def g_copy(h, stage):
        d1, d2 = HALF_BITS[h]
        if stage == 0:
            ref, bit = mine_of(h), d2
        elif stage == 1:
            ref, bit = full[h].at[core, rep_bit(r, d1)], d1
        else:
            ref, bit = full[h].at[core], 0
        return remote(
            ref, ref, g_send.at[h, stage], g_recv.at[h, stage], {"rep": rep_partner(r, bit)}
        )

    gather = [[g_copy(h, s) for h in range(2)] for s in range(BITS)]
    for copy in gather[0]:
        copy.start()
    total = vs[rep_bits]
    qkvb_out[pl.ds(z, 1), :] = total[6:7, :qkv_cols]
    shared = total[:5]
    for t in range(1, group):
        shared = shared + vz[t - 1, :5]
        qkvb_out[pl.ds((z + group - t) % group, 1), :] = vz[t - 1, 6:7, :qkv_cols]
    vec_out[...] = total
    vec_out[:5] = shared
    for s in range(BITS):
        for h in range(2):
            gather[s][h].wait()
            if s + 1 < BITS:
                gather[s + 1][h].start()

    for copy in sums:
        copy.wait()


def finish_kernel(
    group,
    full_a, full_b, sr, parts_ref, x_ref, c_ref, bias_ref,
    y_ref, dx_ref, qkv_out, proj_out, up_out, down_out,
):
    f32, bf16 = jnp.float32, jnp.bfloat16
    z = lax.axis_index("cp")
    rows = x_ref.shape[0]
    own, width = proj_out.shape
    unit = own // SPLIT
    hidden = up_out.shape[1] // group
    qkv_cols = qkv_out.shape[1] // group
    cut = full_a.shape[-1] - hidden
    xs = x_ref[...].astype(f32)
    branch = xs + bias_ref[...]
    scaled = parts_ref[z, rows:].astype(f32)
    branch = branch + parts_ref[z, :rows].astype(f32)
    for t in range(1, group):
        branch = branch + sr[t - 1, :rows].astype(f32)
        scaled = scaled + sr[t - 1, rows:].astype(f32)
    y_ref[...] = branch.astype(bf16)
    center = xs - jnp.mean(xs, axis=-1, keepdims=True)
    inverse = lax.rsqrt(jnp.mean(center * center, axis=-1, keepdims=True) + EPSILON)
    normed = center * inverse
    dx_ref[...] = c_ref[...].astype(f32) + inverse * (
        scaled
        - jnp.mean(scaled, axis=-1, keepdims=True)
        - normed * jnp.mean(scaled * normed, axis=-1, keepdims=True)
    )
    def write(s, carry):
        c0, first, second = s // 4, (s // 2) % 2, s % 2
        base = s * unit
        at = pl.ds(pl.multiple_of(base, 8), unit)
        for u in range(group):
            a = full_a[c0, first, second, u].astype(f32)
            b = full_b[c0, second, first, u].astype(f32)
            up_out[at, u * hidden : (u + 1) * hidden] = a[:, :hidden]
            rows_at = pl.ds(pl.multiple_of(u * own + base, 8), unit)
            down_out[rows_at, :cut] = a[:, hidden:]
            down_out[rows_at, cut:] = b[:, qkv_cols + width // group :]
            proj_out[at, u * (width // group) : (u + 1) * (width // group)] = b[
                :, qkv_cols : qkv_cols + width // group
            ]
            for j in range(3):
                qkv_out[at, j * width + u * own : j * width + (u + 1) * own] = b[
                    :, j * own : (j + 1) * own
                ]
        return carry

    lax.fori_loop(0, SPLIT, write, 0)


def body(
    block_input,
    qkv_weight,
    qkv_bias,
    proj_weight,
    proj_bias,
    up_weight,
    up_bias,
    down_weight,
    down_bias,
    attention_gain,
    attention_shift,
    feed_gain,
    feed_shift,
    out_cotangent,
):
    f32, bf16 = jnp.float32, jnp.bfloat16
    group = lax.axis_size("cp")
    reps = lax.axis_size("rep")
    rank = lax.axis_index("cp")
    rows, width = block_input.shape
    own = width // group
    heads = own // HEAD
    total_rows = rows * group
    hidden = up_weight.shape[1] // group
    qkv_cols = 3 * own
    part_cols = qkv_cols + hidden
    score_scale = HEAD ** (-0.5)

    small = jnp.concatenate(
        [qkv_bias.astype(f32).reshape(3, own)]
        + [
            vector.astype(f32)[None]
            for vector in (
                proj_bias, down_bias, attention_gain, attention_shift, feed_gain, feed_shift
            )
        ],
        axis=0,
    )
    unit = own // SPLIT
    r = lax.axis_index("rep")
    slot = rep_bit(r, 0) * 4 + rep_bit(r, 1) * 2 + rep_bit(r, 2)
    up_piece = (
        lax.dynamic_slice_in_dim(up_weight, slot * unit, unit, axis=0)
        .reshape(unit, group, hidden)
        .transpose(1, 0, 2)
    )
    qkv_piece = (
        lax.dynamic_slice_in_dim(qkv_weight, slot * unit, unit, axis=0)
        .reshape(unit, 3, group, own)
        .transpose(2, 0, 1, 3)
        .reshape(group, unit, qkv_cols)
    )
    vmem = pl.BlockSpec(memory_space=pltpu.VMEM)
    dma = pltpu.SemaphoreType.DMA
    tokens, cotangent, small_all, up_slices, qkv_slices = pl.pallas_call(
        functools.partial(gather_kernel, group, reps),
        out_shape=[
            jax.ShapeDtypeStruct((group, rows, width), bf16),
            jax.ShapeDtypeStruct((group, rows, width), bf16),
            jax.ShapeDtypeStruct((group,) + small.shape, f32),
            jax.ShapeDtypeStruct((2, 2, 2) + up_piece.shape, bf16),
            jax.ShapeDtypeStruct((2, 2, 2) + qkv_piece.shape, bf16),
        ],
        in_specs=[vmem] * 5,
        out_specs=[vmem] * 5,
        scratch_shapes=[
            dma((5,)),
            dma((2, 2, group)),
            dma((2, group)),
            dma((group,)),
            dma((group,)),
            dma((2, group)),
            dma((2, group)),
            dma((2, BITS)),
            dma((2, BITS)),
        ],
        compiler_params=pltpu.CompilerParams(
            collective_id=0, has_side_effects=True, vmem_limit_bytes=50 * 2**20
        ),
    )(block_input, out_cotangent, small, up_piece, qkv_piece)
    tokens = tokens.reshape(total_rows, width)
    cotangent = cotangent.reshape(total_rows, width)
    joined_offset = lax.dynamic_slice_in_dim(
        small_all[:, :3].reshape(3, group, own), rank, 1, axis=1
    ).reshape(qkv_cols)
    proj_offset, down_offset, gain_one, shift_one, gain_two, shift_two = (
        small_all[:, 3 + i].reshape(width) for i in range(6)
    )

    up_matrix = up_slices.transpose(3, 0, 1, 2, 4, 5).reshape(width, hidden)
    joined_matrix = qkv_slices.transpose(3, 0, 2, 1, 4, 5).reshape(width, qkv_cols)

    positions = jnp.arange(total_rows, dtype=jnp.int32)
    cos_table, sin_table = rotary_tables(positions)
    widened = tokens.astype(f32)
    center = widened - jnp.mean(widened, axis=-1, keepdims=True)
    inverse = lax.rsqrt(jnp.mean(center * center, axis=-1, keepdims=True) + EPSILON)
    normed = center * inverse
    attn_in = (normed * gain_one.astype(f32) + shift_one.astype(f32)).astype(bf16)
    feed_in = (normed * gain_two.astype(f32) + shift_two.astype(f32)).astype(bf16)

    joined_out = jnp.dot(attn_in, joined_matrix, preferred_element_type=f32) + joined_offset.astype(
        f32
    )
    queries = rotate(
        joined_out[:, :own].reshape(total_rows, heads, HEAD), cos_table, sin_table
    ).astype(bf16)
    keys = rotate(
        joined_out[:, own : 2 * own].reshape(total_rows, heads, HEAD), cos_table, sin_table
    ).astype(bf16)
    values = joined_out[:, 2 * own :].astype(bf16).reshape(total_rows, heads, HEAD)
    causal = positions[:, None] >= positions[None, :]
    scores = jnp.einsum("thd,shd->hts", queries, keys, preferred_element_type=f32) * score_scale
    scores = jnp.where(causal[None], scores, -jnp.inf)
    top_score = jnp.max(scores, axis=-1, keepdims=True)
    log_total = top_score + jnp.log(jnp.sum(jnp.exp(scores - top_score), axis=-1, keepdims=True))
    exact_probs = jnp.exp(scores - log_total)
    probs_low = exact_probs.astype(bf16)
    context = (
        jnp.einsum("hts,shd->thd", probs_low, values, preferred_element_type=f32)
        .reshape(total_rows, own)
        .astype(bf16)
    )
    pre_act = jnp.dot(feed_in, up_matrix, preferred_element_type=f32) + up_bias.astype(f32)
    activated = (0.5 * pre_act * (1.0 + lax.erf(pre_act * ROOT_HALF))).astype(bf16)
    branch_part = jnp.dot(context, proj_weight, preferred_element_type=f32) + jnp.dot(
        activated, down_weight, preferred_element_type=f32
    )

    bias_sum = jnp.sum(out_cotangent.astype(f32), axis=0, keepdims=True)
    down_grad = jnp.dot(activated.T, cotangent, preferred_element_type=f32)
    pre_grad = jnp.dot(cotangent, down_weight.T, preferred_element_type=f32) * gelu_slope(pre_act)
    pre_low = pre_grad.astype(bf16)
    up_grad = jnp.dot(feed_in.T, pre_low, preferred_element_type=f32)
    up_bgrad = jnp.sum(pre_grad, axis=0, keepdims=True)
    feed_in_grad = jnp.dot(pre_low, up_matrix.T, preferred_element_type=f32)
    proj_grad = jnp.dot(context.T, cotangent, preferred_element_type=f32)
    context_grad = (
        jnp.dot(cotangent, proj_weight.T, preferred_element_type=f32)
        .astype(bf16)
        .reshape(total_rows, heads, HEAD)
    )
    row_dots = jnp.sum(
        context_grad.astype(f32) * context.reshape(total_rows, heads, HEAD).astype(f32), axis=-1
    ).T
    probs_grad = jnp.einsum("thd,shd->hts", context_grad, values, preferred_element_type=f32)
    score_grad = (exact_probs * (probs_grad - row_dots[:, :, None]) * score_scale).astype(bf16)
    query_grad = jnp.einsum("hts,shd->thd", score_grad, keys, preferred_element_type=f32)
    key_grad = jnp.einsum("hts,thd->shd", score_grad, queries, preferred_element_type=f32)
    value_grad = jnp.einsum("hts,thd->shd", probs_low, context_grad, preferred_element_type=f32)
    joined_grad = jnp.concatenate(
        [
            rotate_back(query_grad, cos_table, sin_table).reshape(total_rows, own),
            rotate_back(key_grad, cos_table, sin_table).reshape(total_rows, own),
            value_grad.reshape(total_rows, own),
        ],
        axis=1,
    )
    joined_low = joined_grad.astype(bf16)
    qkv_grad = jnp.dot(attn_in.T, joined_low, preferred_element_type=f32)
    qkv_bgrad = jnp.sum(joined_grad, axis=0, keepdims=True)
    attn_in_grad = jnp.dot(joined_low, joined_matrix.T, preferred_element_type=f32)

    scaled_part = attn_in_grad * gain_one.astype(f32) + feed_in_grad * gain_two.astype(f32)
    parts = jnp.concatenate(
        [branch_part.reshape(group, rows, width), scaled_part.reshape(group, rows, width)], axis=1
    ).astype(bf16)
    bias_row = (proj_offset.astype(f32) + down_offset.astype(f32))[None]

    row_sums = [
        bias_sum,
        jnp.sum(attn_in_grad * normed, axis=0, keepdims=True),
        jnp.sum(attn_in_grad, axis=0, keepdims=True),
        jnp.sum(feed_in_grad * normed, axis=0, keepdims=True),
        jnp.sum(feed_in_grad, axis=0, keepdims=True),
        up_bgrad,
        qkv_bgrad,
    ]
    table = (8, max(width, hidden, qkv_cols))

    rep_bits = reps.bit_length() - 1
    half_w = (qkv_cols + own + width + hidden) // 2
    piece = (group, unit, half_w)
    halves = lambda *lead: [pltpu.VMEM(lead + piece, bf16)] * 2
    spare = max(rep_bits - BITS, 1)
    slices_a, slices_b, received, vectors, qkvb_all = pl.pallas_call(
        functools.partial(reduce_kernel, group, reps, rep_bits),
        out_shape=[
            jax.ShapeDtypeStruct((2, 2, 2) + piece, bf16),
            jax.ShapeDtypeStruct((2, 2, 2) + piece, bf16),
            jax.ShapeDtypeStruct((group - 1, 2 * rows, width), bf16),
            jax.ShapeDtypeStruct(table, f32),
            jax.ShapeDtypeStruct((group, qkv_cols), f32),
        ],
        in_specs=[vmem] * 4 + [[vmem] * 7] + [vmem],
        out_specs=[vmem] * 5,
        scratch_shapes=(
            halves(2, 2, 2)
            + halves(2, 2)
            + halves(2)
            + halves()
            + halves(rep_bits - BITS + 1)
            + halves(spare)
            + [
                pltpu.VMEM((group - 1, unit, hidden), bf16),
                pltpu.VMEM((group - 1, unit, -(-qkv_cols // 128) * 128), bf16),
            ]
            + [
                pltpu.VMEM((rep_bits + 1,) + table, f32),
                pltpu.VMEM((rep_bits,) + table, f32),
                pltpu.VMEM((group - 1,) + table, f32),
                dma((2, BITS)),
                dma((2, BITS)),
                dma((2, spare)),
                dma((2, spare)),
                dma((2, group)),
                dma((2, group)),
                dma((2, BITS)),
                dma((2, BITS)),
                dma((rep_bits,)),
                dma((rep_bits,)),
                dma((group,)),
                dma((group,)),
                dma((2, group)),
                dma((2, group)),
            ]
        ),
        compiler_params=pltpu.CompilerParams(
            collective_id=1, has_side_effects=True, vmem_limit_bytes=60 * 2**20
        ),
    )(
        qkv_grad,
        up_grad,
        proj_grad,
        down_grad,
        row_sums,
        parts,
    )
    block_output, input_grad, qkv_out, proj_out, up_out, down_out = pl.pallas_call(
        functools.partial(finish_kernel, group),
        out_shape=[
            jax.ShapeDtypeStruct((rows, width), bf16),
            jax.ShapeDtypeStruct((rows, width), f32),
            jax.ShapeDtypeStruct((own, group * qkv_cols), f32),
            jax.ShapeDtypeStruct((own, width), f32),
            jax.ShapeDtypeStruct((own, group * hidden), f32),
            jax.ShapeDtypeStruct((hidden, width), f32),
        ],
        in_specs=[vmem] * 7,
        out_specs=[vmem] * 6,
        compiler_params=pltpu.CompilerParams(vmem_limit_bytes=40 * 2**20),
    )(slices_a, slices_b, received, parts, block_input, out_cotangent, bias_row)
    owned = lax.dynamic_slice_in_dim(vectors[:5, :width], rank * own, own, axis=1)
    bias_out, gain1_out, shift1_out, gain2_out, shift2_out = (owned[i] for i in range(5))
    upb_out = vectors[5, :hidden]
    qkvb_out = lax.dynamic_slice_in_dim(
        qkvb_all.reshape(group, 3, own).transpose(1, 0, 2).reshape(-1), rank * qkv_cols, qkv_cols
    )
    return (
        block_output,
        input_grad,
        qkv_out,
        qkvb_out,
        proj_out,
        bias_out,
        up_out,
        upb_out,
        down_out,
        bias_out,
        gain1_out,
        shift1_out,
        gain2_out,
        shift2_out,
    )


def solution(mesh):
    return jax.shard_map(
        body,
        mesh=mesh,
        in_specs=(
            P(("rep", "cp"), None),
            P("cp", None),
            P("cp"),
            P("cp", None),
            P("cp"),
            P("cp", None),
            P("cp"),
            P("cp", None),
            P("cp"),
            P("cp"),
            P("cp"),
            P("cp"),
            P("cp"),
            P(("rep", "cp"), None),
        ),
        out_specs=(
            P(("rep", "cp"), None),
            P(("rep", "cp"), None),
            P("cp", None),
            P("cp"),
            P("cp", None),
            P("cp"),
            P("cp", None),
            P("cp"),
            P("cp", None),
            P("cp"),
            P("cp"),
            P("cp"),
            P("cp"),
            P("cp"),
        ),
        check_vma=False,
    )
```

```python
import functools

import jax
import jax.numpy as jnp
from jax import lax
from jax.experimental import pallas as pl
from jax.experimental.pallas import tpu as pltpu
from jax.sharding import PartitionSpec as P

HEAD = 64
ROT = 16


EPSILON = 1e-05
ROOT_HALF = 0.7071067811865476
INV_ROOT_TWO_PI = 0.3989422804014327


def layer_norm(inputs, norm_gain, norm_shift):
    center = inputs - jnp.mean(inputs, axis=-1, keepdims=True)
    inverse = lax.rsqrt(jnp.mean(center * center, axis=-1, keepdims=True) + EPSILON)
    normed = center * inverse
    return (
        normed * norm_gain.astype(jnp.float32) + norm_shift.astype(jnp.float32),
        normed,
        inverse,
    )


def norm_back(upstream, normed, inverse, norm_gain):
    scaled = upstream * norm_gain.astype(jnp.float32)
    return inverse * (
        scaled
        - jnp.mean(scaled, axis=-1, keepdims=True)
        - normed * jnp.mean(scaled * normed, axis=-1, keepdims=True)
    )


def rotary_tables(positions):
    half_rot = ROT // 2
    inverse_freq = 1.0 / 10000.0 ** (jnp.arange(half_rot, dtype=jnp.float32) * (2.0 / ROT))
    angles = positions.astype(jnp.float32)[:, None] * inverse_freq[None, :]
    cos_table = jnp.concatenate([jnp.cos(angles), jnp.cos(angles)], axis=-1)
    sin_table = jnp.concatenate([jnp.sin(angles), jnp.sin(angles)], axis=-1)
    return (cos_table, sin_table)


def rotate(heads_in, cos_table, sin_table):
    half_rot = ROT // 2
    rotary_part = heads_in[..., :ROT]
    turned = jnp.concatenate([-rotary_part[..., half_rot:], rotary_part[..., :half_rot]], axis=-1)
    rotated = rotary_part * cos_table[:, None, :] + turned * sin_table[:, None, :]
    return jnp.concatenate([rotated, heads_in[..., ROT:]], axis=-1)


def rotate_back(heads_grad, cos_table, sin_table):
    half_rot = ROT // 2
    sined = heads_grad[..., :ROT] * sin_table[:, None, :]
    swapped = jnp.concatenate([sined[..., half_rot:], -sined[..., :half_rot]], axis=-1)
    rotated = heads_grad[..., :ROT] * cos_table[:, None, :] + swapped
    return jnp.concatenate([rotated, heads_grad[..., ROT:]], axis=-1)


def gelu_slope(preact):
    return (
        0.5 * (1.0 + lax.erf(preact * ROOT_HALF))
        + preact * jnp.exp(-0.5 * preact * preact) * INV_ROOT_TWO_PI
    )

SPLIT = 8
BITS = 3


def rep_bit(r, k):
    return (r // (1 << k)) % 2


def rep_partner(r, k):
    return r + (1 << k) * (1 - 2 * rep_bit(r, k))


def greet(group, reps, z, r, rep_bits):
    barrier = pltpu.get_barrier_semaphore()
    for t in range(1, group):
        pl.semaphore_signal(barrier, inc=1, device_id={"cp": (z + t) % group})
    for k in range(rep_bits):
        pl.semaphore_signal(barrier, inc=1, device_id={"rep": rep_partner(r, k)})
    pl.semaphore_wait(barrier, group - 1 + rep_bits)


def remote(src, dst, send, recv, device):
    return pltpu.make_async_remote_copy(
        src_ref=src, dst_ref=dst, send_sem=send, recv_sem=recv, device_id=device
    )


HALF_BITS = ((1, 2), (2, 1))


def gather_kernel(
    group, reps,
    x_ref, c_ref, s_ref, pu_ref, pq_ref,
    xa_ref, ca_ref, sa_ref, cu_ref, cq_ref,
    loc_sem, line_send, line_recv, small_send, small_recv, z_send, z_recv, g_send, g_recv,
):
    z = lax.axis_index("cp")
    r = lax.axis_index("rep")
    greet(group, reps, z, r, BITS)
    core = rep_bit(r, 0)
    pieces = (pu_ref, pq_ref)
    full = (cu_ref, cq_ref)

    def own(h):
        d1, d2 = HALF_BITS[h]
        return full[h].at[core, rep_bit(r, d1), rep_bit(r, d2)]

    waits = []
    for h in range(2):
        for t in range(1, group):
            to = (z + t) % group
            copy = remote(
                pieces[h].at[to], own(h).at[z], z_send.at[h, t], z_recv.at[h, t], {"cp": to}
            )
            copy.start()
            waits.append(copy)
    for t in range(1, group):
        copy = remote(
            s_ref, sa_ref.at[z], small_send.at[t], small_recv.at[t], {"cp": (z + t) % group}
        )
        copy.start()
        waits.append(copy)
    lines = ((x_ref, xa_ref), (c_ref, ca_ref))

    def line_copy(i, source, direction, first):
        src = lines[i][0] if first else lines[i][1].at[source]
        return remote(
            src,
            lines[i][1].at[source],
            line_send.at[i, direction, source],
            line_recv.at[i, source],
            {"cp": z + 1 - 2 * direction},
        )

    for i in range(2):
        @pl.when(z < group - 1)
        def _():
            line_copy(i, z, 0, True).start()

        @pl.when(z > 0)
        def _():
            line_copy(i, z, 1, True).start()
    locals_ = [
        pltpu.make_async_copy(x_ref, xa_ref.at[z], loc_sem.at[0]),
        pltpu.make_async_copy(c_ref, ca_ref.at[z], loc_sem.at[1]),
        pltpu.make_async_copy(s_ref, sa_ref.at[z], loc_sem.at[2]),
        pltpu.make_async_copy(pu_ref.at[z], own(0).at[z], loc_sem.at[3]),
        pltpu.make_async_copy(pq_ref.at[z], own(1).at[z], loc_sem.at[4]),
    ]
    for copy in locals_:
        copy.start()
    for copy in locals_:
        copy.wait()

    for copy in waits:
        copy.wait()

    def stage_copy(h, stage):
        d1, d2 = HALF_BITS[h]
        if stage == 0:
            ref, bit = own(h), d2
        elif stage == 1:
            ref, bit = full[h].at[core, rep_bit(r, d1)], d1
        else:
            ref, bit = full[h].at[core], 0
        return remote(
            ref, ref, g_send.at[h, stage], g_recv.at[h, stage], {"rep": rep_partner(r, bit)}
        )

    def step(t):
        for i in range(2):
            @pl.when(z >= t)
            def _():
                line_copy(i, z - t, 0, False).wait_recv()

                @pl.when(z < group - 1)
                def _():
                    line_copy(i, z - t, 0, False).start()

            @pl.when(z + t < group)
            def _():
                line_copy(i, z + t, 1, False).wait_recv()

                @pl.when(z > 0)
                def _():
                    line_copy(i, z + t, 1, False).start()

    stages = [[stage_copy(h, s) for h in range(2)] for s in range(BITS)]
    for copy in stages[0]:
        copy.start()
    for s in range(BITS):
        for copy in stages[s]:
            copy.wait()
        if s + 1 < BITS:
            for copy in stages[s + 1]:
                copy.start()
        if s + 1 < group:
            step(s + 1)
    for t in range(BITS + 1, group):
        step(t)
    for i in range(2):
        for t in range(group):
            @pl.when((z >= t) & (z < group - 1))
            def _():
                line_copy(i, z - t, 0, t == 0).wait_send()

            @pl.when((z + t < group) & (z > 0))
            def _():
                line_copy(i, z + t, 1, t == 0).wait_send()


def reduce_kernel(
    group, reps, rep_bits,
    qkv_ref, up_ref, proj_ref, down_ref, sum_refs, parts_ref,
    full_a, full_b, sr, vec_out, qkvb_out,
    buf_a, buf_b, r0_a, r0_b, r1_a, r1_b, r2_a, r2_b, up_send_a, up_send_b, ru_a, ru_b,
    zr_a, zr_b, vs, vr, vz,
    rs_send, rs_recv, u_send, u_recv, z_send, z_recv, g_send, g_recv,
    v_send, v_recv, vz_send, vz_recv, s_send, s_recv,
):
    f32, bf16 = jnp.float32, jnp.bfloat16
    z = lax.axis_index("cp")
    r = lax.axis_index("rep")
    greet(group, reps, z, r, rep_bits)
    core = rep_bit(r, 0)
    rows = parts_ref.shape[1] // 2
    own, width = proj_ref.shape
    unit = own // SPLIT
    hidden = up_ref.shape[1]
    qkv_cols = qkv_ref.shape[1]
    half_w = buf_a.shape[-1]
    cut = half_w - hidden
    buf = (buf_a, buf_b)
    r0 = (r0_a, r0_b)
    r1 = (r1_a, r1_b)
    r2 = (r2_a, r2_b)
    up_send = (up_send_a, up_send_b)
    ru = (ru_a, ru_b)
    zr = (zr_a, zr_b)
    full = (full_a, full_b)
    zw = (zr_a.shape[-1], zr_b.shape[-1])

    sums = []
    for i in range(2):
        for t in range(1, group):
            to = (z + t) % group
            at = pl.ds(i * rows, rows)
            sums.append(
                remote(
                    parts_ref.at[to, at],
                    sr.at[t - 1, at],
                    s_send.at[i, t],
                    s_recv.at[i, t],
                    {"cp": to},
                )
            )

    def fill(s, core_bit):
        first, second = s // 2, s % 2
        base = (core_bit * 4 + s) * unit
        proj = proj_ref[pl.ds(pl.multiple_of(base, 8), unit), :].astype(bf16)
        for u in range(group):
            at = pl.ds(pl.multiple_of(u * own + base, 8), unit)
            down = down_ref[at, :].astype(bf16)
            buf_a[core_bit, first, second, u] = jnp.concatenate(
                [up_ref[at, :].astype(bf16), down[:, :cut]], axis=1
            )
            buf_b[core_bit, second, first, u] = jnp.concatenate(
                [
                    qkv_ref[at, :].astype(bf16),
                    proj[:, u * (width // group) : (u + 1) * (width // group)],
                    down[:, cut:],
                ],
                axis=1,
            )

    def fill_loop(core_bit):
        lax.fori_loop(0, 4, lambda s, n: (fill(s, core_bit), n)[1], 0)

    def rs_copy(h, stage):
        d1, d2 = HALF_BITS[h]
        if stage == 0:
            src, dst, bit = buf[h].at[1 - core], r0[h], 0
        elif stage == 1:
            src, dst, bit = r0[h].at[1 - rep_bit(r, d1)], r1[h], d1
        else:
            src, dst, bit = r1[h].at[1 - rep_bit(r, d2)], r2[h], d2
        return remote(
            src, dst, rs_send.at[h, stage], rs_recv.at[h, stage], {"rep": rep_partner(r, bit)}
        )

    def v_copy(k):
        return remote(
            vs.at[k], vr.at[k], v_send.at[k], v_recv.at[k], {"rep": rep_partner(r, k)}
        )

    for copy in sums[: group - 1]:
        copy.start()
    fill_loop(1 - core)
    rs = [[rs_copy(h, s) for h in range(2)] for s in range(BITS)]
    for copy in rs[0]:
        copy.start()
    vs[0] = jnp.zeros(vs.shape[1:], f32)
    for i, ref in enumerate(sum_refs):
        vs[0, i, : ref.shape[0]] = ref[...]
    v_copy(0).start()
    fill_loop(core)

    for h in range(2):
        rs[0][h].wait()

        def add0(n, carry):
            a, b, u = n // (2 * group), (n // group) % 2, n % group
            r0[h][a, b, u] = (
                r0[h][a, b, u].astype(f32) + buf[h][core, a, b, u].astype(f32)
            ).astype(bf16)
            return carry

        lax.fori_loop(0, 4 * group, add0, 0)
        rs[1][h].start()
    v_copy(0).wait()
    vs[1] = vs[0] + vr[0]
    v_copy(1).start()
    for h in range(2):
        rs[1][h].wait()
        mine = rep_bit(r, HALF_BITS[h][0])

        def add1(n, carry):
            b, u = n // group, n % group
            r1[h][b, u] = (
                r1[h][b, u].astype(f32) + r0[h][mine, b, u].astype(f32)
            ).astype(bf16)
            return carry

        lax.fori_loop(0, 2 * group, add1, 0)
        rs[2][h].start()
    v_copy(1).wait()
    vs[2] = vs[1] + vr[1]
    v_copy(2).start()
    for h in range(2):
        rs[2][h].wait()
        mine = rep_bit(r, HALF_BITS[h][1])
        for u in range(group):
            up_send[h][0, u] = (
                r2[h][u].astype(f32) + r1[h][mine, u].astype(f32)
            ).astype(bf16)
    v_copy(2).wait()
    vs[3] = vs[2] + vr[2]
    for k in range(BITS, rep_bits):
        copies = [
            remote(
                up_send[h].at[k - BITS],
                ru[h].at[k - BITS],
                u_send.at[h, k - BITS],
                u_recv.at[h, k - BITS],
                {"rep": rep_partner(r, k)},
            )
            for h in range(2)
        ] + [v_copy(k)]
        for copy in copies:
            copy.start()
        for copy in copies:
            copy.wait()
        for h in range(2):
            up_send[h][k - BITS + 1] = (
                up_send[h][k - BITS].astype(f32) + ru[h][k - BITS].astype(f32)
            ).astype(bf16)
        vs[k + 1] = vs[k] + vr[k]
    last = rep_bits - BITS
    final = [up_send[h].at[last] for h in range(2)]
    exchange = []
    for t in range(1, group):
        to = (z + t) % group
        for h in range(2):
            exchange.append(
                remote(
                    final[h].at[to, :, pl.ds(0, zw[h])],
                    zr[h].at[t - 1],
                    z_send.at[h, t],
                    z_recv.at[h, t],
                    {"cp": to},
                )
            )
        exchange.append(
            remote(
                vs.at[rep_bits], vz.at[t - 1], vz_send.at[t], vz_recv.at[t], {"cp": to}
            )
        )
    for copy in exchange:
        copy.start()
    for copy in sums[group - 1 :]:
        copy.start()

    def mine_of(h):
        d1, d2 = HALF_BITS[h]
        return full[h].at[core, rep_bit(r, d1), rep_bit(r, d2)]

    for copy in exchange:
        copy.wait()
    used = (hidden, qkv_cols)
    for h in range(2):
        piece = mine_of(h)
        for u in range(group):
            piece[u, :, used[h] :] = final[h][u, :, used[h] :]
        piece[z, :, : used[h]] = final[h][z, :, : used[h]]
        for t in range(1, group):
            piece[(z + group - t) % group, :, : used[h]] = zr[h][t - 1][:, : used[h]]
    def g_copy(h, stage):
        d1, d2 = HALF_BITS[h]
        if stage == 0:
            ref, bit = mine_of(h), d2
        elif stage == 1:
            ref, bit = full[h].at[core, rep_bit(r, d1)], d1
        else:
            ref, bit = full[h].at[core], 0
        return remote(
            ref, ref, g_send.at[h, stage], g_recv.at[h, stage], {"rep": rep_partner(r, bit)}
        )

    gather = [[g_copy(h, s) for h in range(2)] for s in range(BITS)]
    for copy in gather[0]:
        copy.start()
    total = vs[rep_bits]
    qkvb_out[pl.ds(z, 1), :] = total[6:7, :qkv_cols]
    shared = total[:5]
    for t in range(1, group):
        shared = shared + vz[t - 1, :5]
        qkvb_out[pl.ds((z + group - t) % group, 1), :] = vz[t - 1, 6:7, :qkv_cols]
    vec_out[...] = total
    vec_out[:5] = shared
    for s in range(BITS):
        for h in range(2):
            gather[s][h].wait()
            if s + 1 < BITS:
                gather[s + 1][h].start()

    for copy in sums:
        copy.wait()


def finish_kernel(
    group,
    full_a, full_b, sr, parts_ref, x_ref, c_ref, bias_ref,
    y_ref, dx_ref, qkv_out, proj_out, up_out, down_out,
):
    f32, bf16 = jnp.float32, jnp.bfloat16
    z = lax.axis_index("cp")
    rows = x_ref.shape[0]
    own, width = proj_out.shape
    unit = own // SPLIT
    hidden = up_out.shape[1] // group
    qkv_cols = qkv_out.shape[1] // group
    cut = full_a.shape[-1] - hidden
    xs = x_ref[...].astype(f32)
    branch = xs + bias_ref[...]
    scaled = parts_ref[z, rows:].astype(f32)
    branch = branch + parts_ref[z, :rows].astype(f32)
    for t in range(1, group):
        branch = branch + sr[t - 1, :rows].astype(f32)
        scaled = scaled + sr[t - 1, rows:].astype(f32)
    y_ref[...] = branch.astype(bf16)
    center = xs - jnp.mean(xs, axis=-1, keepdims=True)
    inverse = lax.rsqrt(jnp.mean(center * center, axis=-1, keepdims=True) + EPSILON)
    normed = center * inverse
    dx_ref[...] = c_ref[...].astype(f32) + inverse * (
        scaled
        - jnp.mean(scaled, axis=-1, keepdims=True)
        - normed * jnp.mean(scaled * normed, axis=-1, keepdims=True)
    )
    def write(s, carry):
        c0, first, second = s // 4, (s // 2) % 2, s % 2
        base = s * unit
        at = pl.ds(pl.multiple_of(base, 8), unit)
        for u in range(group):
            a = full_a[c0, first, second, u].astype(f32)
            b = full_b[c0, second, first, u].astype(f32)
            up_out[at, u * hidden : (u + 1) * hidden] = a[:, :hidden]
            rows_at = pl.ds(pl.multiple_of(u * own + base, 8), unit)
            down_out[rows_at, :cut] = a[:, hidden:]
            down_out[rows_at, cut:] = b[:, qkv_cols + width // group :]
            proj_out[at, u * (width // group) : (u + 1) * (width // group)] = b[
                :, qkv_cols : qkv_cols + width // group
            ]
            for j in range(3):
                qkv_out[at, j * width + u * own : j * width + (u + 1) * own] = b[
                    :, j * own : (j + 1) * own
                ]
        return carry

    lax.fori_loop(0, SPLIT, write, 0)


def body(
    block_input,
    qkv_weight,
    qkv_bias,
    proj_weight,
    proj_bias,
    up_weight,
    up_bias,
    down_weight,
    down_bias,
    attention_gain,
    attention_shift,
    feed_gain,
    feed_shift,
    out_cotangent,
):
    f32, bf16 = jnp.float32, jnp.bfloat16
    group = lax.axis_size("cp")
    reps = lax.axis_size("rep")
    rank = lax.axis_index("cp")
    rows, width = block_input.shape
    own = width // group
    heads = own // HEAD
    total_rows = rows * group
    hidden = up_weight.shape[1] // group
    qkv_cols = 3 * own
    part_cols = qkv_cols + hidden
    score_scale = HEAD ** (-0.5)

    small = jnp.concatenate(
        [qkv_bias.astype(f32).reshape(3, own)]
        + [
            vector.astype(f32)[None]
            for vector in (
                proj_bias, down_bias, attention_gain, attention_shift, feed_gain, feed_shift
            )
        ],
        axis=0,
    )
    unit = own // SPLIT
    r = lax.axis_index("rep")
    slot = rep_bit(r, 0) * 4 + rep_bit(r, 1) * 2 + rep_bit(r, 2)
    up_piece = (
        lax.dynamic_slice_in_dim(up_weight, slot * unit, unit, axis=0)
        .reshape(unit, group, hidden)
        .transpose(1, 0, 2)
    )
    qkv_piece = (
        lax.dynamic_slice_in_dim(qkv_weight, slot * unit, unit, axis=0)
        .reshape(unit, 3, group, own)
        .transpose(2, 0, 1, 3)
        .reshape(group, unit, qkv_cols)
    )
    vmem = pl.BlockSpec(memory_space=pltpu.VMEM)
    dma = pltpu.SemaphoreType.DMA
    tokens, cotangent, small_all, up_slices, qkv_slices = pl.pallas_call(
        functools.partial(gather_kernel, group, reps),
        out_shape=[
            jax.ShapeDtypeStruct((group, rows, width), bf16),
            jax.ShapeDtypeStruct((group, rows, width), bf16),
            jax.ShapeDtypeStruct((group,) + small.shape, f32),
            jax.ShapeDtypeStruct((2, 2, 2) + up_piece.shape, bf16),
            jax.ShapeDtypeStruct((2, 2, 2) + qkv_piece.shape, bf16),
        ],
        in_specs=[vmem] * 5,
        out_specs=[vmem] * 5,
        scratch_shapes=[
            dma((5,)),
            dma((2, 2, group)),
            dma((2, group)),
            dma((group,)),
            dma((group,)),
            dma((2, group)),
            dma((2, group)),
            dma((2, BITS)),
            dma((2, BITS)),
        ],
        compiler_params=pltpu.CompilerParams(
            collective_id=0, has_side_effects=True, vmem_limit_bytes=50 * 2**20
        ),
    )(block_input, out_cotangent, small, up_piece, qkv_piece)
    tokens = tokens.reshape(total_rows, width)
    cotangent = cotangent.reshape(total_rows, width)
    joined_offset = lax.dynamic_slice_in_dim(
        small_all[:, :3].reshape(3, group, own), rank, 1, axis=1
    ).reshape(qkv_cols)
    proj_offset, down_offset, gain_one, shift_one, gain_two, shift_two = (
        small_all[:, 3 + i].reshape(width) for i in range(6)
    )

    up_matrix = up_slices.transpose(3, 0, 1, 2, 4, 5).reshape(width, hidden)
    joined_matrix = qkv_slices.transpose(3, 0, 2, 1, 4, 5).reshape(width, qkv_cols)

    positions = jnp.arange(total_rows, dtype=jnp.int32)
    cos_table, sin_table = rotary_tables(positions)
    widened = tokens.astype(f32)
    center = widened - jnp.mean(widened, axis=-1, keepdims=True)
    inverse = lax.rsqrt(jnp.mean(center * center, axis=-1, keepdims=True) + EPSILON)
    normed = center * inverse
    attn_in = (normed * gain_one.astype(f32) + shift_one.astype(f32)).astype(bf16)
    feed_in = (normed * gain_two.astype(f32) + shift_two.astype(f32)).astype(bf16)

    joined_out = jnp.dot(attn_in, joined_matrix, preferred_element_type=f32) + joined_offset.astype(
        f32
    )
    queries = rotate(
        joined_out[:, :own].reshape(total_rows, heads, HEAD), cos_table, sin_table
    ).astype(bf16)
    keys = rotate(
        joined_out[:, own : 2 * own].reshape(total_rows, heads, HEAD), cos_table, sin_table
    ).astype(bf16)
    values = joined_out[:, 2 * own :].astype(bf16).reshape(total_rows, heads, HEAD)
    causal = positions[:, None] >= positions[None, :]
    scores = jnp.einsum("thd,shd->hts", queries, keys, preferred_element_type=f32) * score_scale
    scores = jnp.where(causal[None], scores, -jnp.inf)
    top_score = jnp.max(scores, axis=-1, keepdims=True)
    log_total = top_score + jnp.log(jnp.sum(jnp.exp(scores - top_score), axis=-1, keepdims=True))
    exact_probs = jnp.exp(scores - log_total)
    probs_low = exact_probs.astype(bf16)
    context = (
        jnp.einsum("hts,shd->thd", probs_low, values, preferred_element_type=f32)
        .reshape(total_rows, own)
        .astype(bf16)
    )
    pre_act = jnp.dot(feed_in, up_matrix, preferred_element_type=f32) + up_bias.astype(f32)
    activated = (0.5 * pre_act * (1.0 + lax.erf(pre_act * ROOT_HALF))).astype(bf16)
    branch_part = jnp.dot(context, proj_weight, preferred_element_type=f32) + jnp.dot(
        activated, down_weight, preferred_element_type=f32
    )

    bias_sum = jnp.sum(out_cotangent.astype(f32), axis=0)
    down_grad = jnp.dot(activated.T, cotangent, preferred_element_type=f32)
    pre_grad = jnp.dot(cotangent, down_weight.T, preferred_element_type=f32) * gelu_slope(pre_act)
    pre_low = pre_grad.astype(bf16)
    up_grad = jnp.dot(feed_in.T, pre_low, preferred_element_type=f32)
    up_bgrad = jnp.sum(pre_grad, axis=0)
    feed_in_grad = jnp.dot(pre_low, up_matrix.T, preferred_element_type=f32)
    proj_grad = jnp.dot(context.T, cotangent, preferred_element_type=f32)
    context_grad = (
        jnp.dot(cotangent, proj_weight.T, preferred_element_type=f32)
        .astype(bf16)
        .reshape(total_rows, heads, HEAD)
    )
    row_dots = jnp.sum(
        context_grad.astype(f32) * context.reshape(total_rows, heads, HEAD).astype(f32), axis=-1
    ).T
    probs_grad = jnp.einsum("thd,shd->hts", context_grad, values, preferred_element_type=f32)
    score_grad = (exact_probs * (probs_grad - row_dots[:, :, None]) * score_scale).astype(bf16)
    query_grad = jnp.einsum("hts,shd->thd", score_grad, keys, preferred_element_type=f32)
    key_grad = jnp.einsum("hts,thd->shd", score_grad, queries, preferred_element_type=f32)
    value_grad = jnp.einsum("hts,thd->shd", probs_low, context_grad, preferred_element_type=f32)
    joined_grad = jnp.concatenate(
        [
            rotate_back(query_grad, cos_table, sin_table).reshape(total_rows, own),
            rotate_back(key_grad, cos_table, sin_table).reshape(total_rows, own),
            value_grad.reshape(total_rows, own),
        ],
        axis=1,
    )
    joined_low = joined_grad.astype(bf16)
    qkv_grad = jnp.dot(attn_in.T, joined_low, preferred_element_type=f32)
    qkv_bgrad = jnp.sum(joined_grad, axis=0)
    attn_in_grad = jnp.dot(joined_low, joined_matrix.T, preferred_element_type=f32)

    scaled_part = attn_in_grad * gain_one.astype(f32) + feed_in_grad * gain_two.astype(f32)
    parts = jnp.concatenate(
        [branch_part.reshape(group, rows, width), scaled_part.reshape(group, rows, width)], axis=1
    ).astype(bf16)
    bias_row = (proj_offset.astype(f32) + down_offset.astype(f32))[None]

    row_sums = [
        bias_sum,
        jnp.sum(attn_in_grad * normed, axis=0),
        jnp.sum(attn_in_grad, axis=0),
        jnp.sum(feed_in_grad * normed, axis=0),
        jnp.sum(feed_in_grad, axis=0),
        up_bgrad,
        qkv_bgrad,
    ]
    table = (8, max(width, hidden, qkv_cols))

    rep_bits = reps.bit_length() - 1
    half_w = (qkv_cols + own + width + hidden) // 2
    piece = (group, unit, half_w)
    halves = lambda *lead: [pltpu.VMEM(lead + piece, bf16)] * 2
    spare = max(rep_bits - BITS, 1)
    slices_a, slices_b, received, vectors, qkvb_all = pl.pallas_call(
        functools.partial(reduce_kernel, group, reps, rep_bits),
        out_shape=[
            jax.ShapeDtypeStruct((2, 2, 2) + piece, bf16),
            jax.ShapeDtypeStruct((2, 2, 2) + piece, bf16),
            jax.ShapeDtypeStruct((group - 1, 2 * rows, width), bf16),
            jax.ShapeDtypeStruct(table, f32),
            jax.ShapeDtypeStruct((group, qkv_cols), f32),
        ],
        in_specs=[vmem] * 4 + [[vmem] * 7] + [vmem],
        out_specs=[vmem] * 5,
        scratch_shapes=(
            halves(2, 2, 2)
            + halves(2, 2)
            + halves(2)
            + halves()
            + halves(rep_bits - BITS + 1)
            + halves(spare)
            + [
                pltpu.VMEM((group - 1, unit, hidden), bf16),
                pltpu.VMEM((group - 1, unit, -(-qkv_cols // 128) * 128), bf16),
            ]
            + [
                pltpu.VMEM((rep_bits + 1,) + table, f32),
                pltpu.VMEM((rep_bits,) + table, f32),
                pltpu.VMEM((group - 1,) + table, f32),
                dma((2, BITS)),
                dma((2, BITS)),
                dma((2, spare)),
                dma((2, spare)),
                dma((2, group)),
                dma((2, group)),
                dma((2, BITS)),
                dma((2, BITS)),
                dma((rep_bits,)),
                dma((rep_bits,)),
                dma((group,)),
                dma((group,)),
                dma((2, group)),
                dma((2, group)),
            ]
        ),
        compiler_params=pltpu.CompilerParams(
            collective_id=1, has_side_effects=True, vmem_limit_bytes=60 * 2**20
        ),
    )(
        qkv_grad,
        up_grad,
        proj_grad,
        down_grad,
        row_sums,
        parts,
    )
    block_output, input_grad, qkv_out, proj_out, up_out, down_out = pl.pallas_call(
        functools.partial(finish_kernel, group),
        out_shape=[
            jax.ShapeDtypeStruct((rows, width), bf16),
            jax.ShapeDtypeStruct((rows, width), f32),
            jax.ShapeDtypeStruct((own, group * qkv_cols), f32),
            jax.ShapeDtypeStruct((own, width), f32),
            jax.ShapeDtypeStruct((own, group * hidden), f32),
            jax.ShapeDtypeStruct((hidden, width), f32),
        ],
        in_specs=[vmem] * 7,
        out_specs=[vmem] * 6,
        compiler_params=pltpu.CompilerParams(vmem_limit_bytes=40 * 2**20),
    )(slices_a, slices_b, received, parts, block_input, out_cotangent, bias_row)
    owned = lax.dynamic_slice_in_dim(vectors[:5, :width], rank * own, own, axis=1)
    bias_out, gain1_out, shift1_out, gain2_out, shift2_out = (owned[i] for i in range(5))
    upb_out = vectors[5, :hidden]
    qkvb_out = lax.dynamic_slice_in_dim(
        qkvb_all.reshape(group, 3, own).transpose(1, 0, 2).reshape(-1), rank * qkv_cols, qkv_cols
    )
    return (
        block_output,
        input_grad,
        qkv_out,
        qkvb_out,
        proj_out,
        bias_out,
        up_out,
        upb_out,
        down_out,
        bias_out,
        gain1_out,
        shift1_out,
        gain2_out,
        shift2_out,
    )


def solution(mesh):
    return jax.shard_map(
        body,
        mesh=mesh,
        in_specs=(
            P(("rep", "cp"), None),
            P("cp", None),
            P("cp"),
            P("cp", None),
            P("cp"),
            P("cp", None),
            P("cp"),
            P("cp", None),
            P("cp"),
            P("cp"),
            P("cp"),
            P("cp"),
            P("cp"),
            P(("rep", "cp"), None),
        ),
        out_specs=(
            P(("rep", "cp"), None),
            P(("rep", "cp"), None),
            P("cp", None),
            P("cp"),
            P("cp", None),
            P("cp"),
            P("cp", None),
            P("cp"),
            P("cp", None),
            P("cp"),
            P("cp"),
            P("cp"),
            P("cp"),
            P("cp"),
        ),
        check_vma=False,
    )
```
